32 devices in a mesh: groups: 2 (over x), wide: 16 (over z, y, core).
Axes of the slice: x: 2, y: 2, z: 4, core: 2. Of those that a mesh axis runs over, the one named last changes fastest.
Arguments:
- queries: bfloat16 [4096, 512], P(('groups', 'wide')), parts along dimension 0, may hold values from -200 to 200, as said below
- tree_kv: bfloat16 [2, 4096, 128], P(None, ('groups', 'wide')), parts along dimension 1, may hold values from -7 to 7, as said below
- kv_cache: bfloat16 [2, 512, 32, 128], P(None, ('groups', 'wide')), parts along dimension 1, may hold values from -6 to 6, as said below
- block_table: int32 [128, 4], P(('groups', 'wide')), parts along dimension 0, may hold values from 0 to 15, as said below
- cache_lengths: int32 [32, 4], P(('groups', 'wide')), parts along dimension 0, may hold values from 1 to 128, as said below
- parents: int32 [128, 32], P(('groups', 'wide')), parts along dimension 0, may hold values from -1 to 30, as said below
- w_out: bfloat16 [8192, 2048], P('wide'), may hold values from -0.375 to 0.375, as said below
- w_gate: bfloat16 [16, 2048, 768], P('wide'), may hold values from -0.125 to 0.125
- w_up: bfloat16 [16, 2048, 768], P('wide'), may hold values from -0.125 to 0.125
- w_down: bfloat16 [16, 768, 2048], P('wide'), may hold values from -0.4375 to 0.4375
- expert_ids: int32 [512, 8], P(('groups', 'wide')), parts along dimension 0, may hold values from 0 to 15, as said below
- gate_weights: float32 [512, 8], P(('groups', 'wide')), parts along dimension 0, may hold values from 0.05 to 0.5
Outputs:
- mixed: bfloat16 [512, 2048], P(('groups', 'wide')), parts along dimension 0
The draws below stay inside these ranges and needn't reach their ends.
There are 2 independent parts, one for each index of `groups`. The reference program is written for one: setup_inputs(seed, part) draws one part's arguments, and reference() takes and returns one part's arrays. A program takes and returns all parts, laid end to end along the dimension named above; an argument that names none is the same for every part. Nothing has to cross between parts.
Inputs may be any that keep to these rules, and one draw needn't show every extreme that they name: `queries`: its hidden draw may carry large entries. `tree_kv`: blocks of one group whose slices use the same key head are equal. `kv_cache`: pools of one group whose slices use the same key head are equal. `block_table`: each device's rows list every page of its pool once; blocks t * 2 + g are equal for all t. `cache_lengths`: rows t * 2 + g are equal for all t; every row holds one length 128 and one length 1. `parents`: node i of a tree has a parent before it; node 0 is the root with parent -1; blocks t * 2 + g are equal for all t. `w_out`: blocks of one head slice are equal. `expert_ids`: each row lists 8 different experts. Within the rows of one device no expert is listed by more than 10 rows; in every draw one expert is listed by exactly 10 rows of every device.
All inputs are finite; a program needn't handle non-finite values.
Results may differ from the reference program's by a relative error of at most 0.0083.
Values may be sent and summed in bfloat16 or wider, within the bound.
A program may use at most 64 MiB of HBM per device.

```python
import math
import jax
import jax.numpy as jnp
from jax import lax

D_MODEL = 2048
KV_HEADS = 4
HEAD_DIM = 128
FF_EXP = 768
TOP_K = 8
EXPERTS = 16
ATT_TP = 8
QH_DEV = 4
HEAD_SLICE = 512
GROUPS = 2
TREE_ROWS = 32
GROUP_SEQS = 4
PAGE_LEN = 32
PAGES_SEQ = 4
CACHE_MAX = 128
POOL_DEV = 16
ROWS_G = 128
ROWS_DEV = 16
TOKENS = 256
MEAN_LOAD = 8
MOST_ROWS = 10
N_WIDE = 16


def device_heads():
    devices = jnp.arange(ATT_TP * GROUPS, dtype=jnp.int32)
    return (devices // GROUPS // (ATT_TP // KV_HEADS), devices % GROUPS)


def by_group(base):
    return jnp.tile(base, (ATT_TP,) + (1,) * (base.ndim - 1))


def node_keys(key):
    source = jax.random.fold_in(key, 7001)
    return jnp.clip(jax.random.normal(source, (KV_HEADS, GROUPS, ROWS_G, HEAD_DIM), jnp.float32), -6.0, 6.0)


def draw_tree_kv(key, part):
    key_rows = node_keys(key)
    value_rows = jnp.clip(jax.random.normal(jax.random.fold_in(key, 7002), (KV_HEADS, GROUPS, ROWS_G, HEAD_DIM), jnp.float32), -6.0, 6.0)
    head_ids, group_ids = device_heads()
    stacked = jnp.stack([key_rows[head_ids, group_ids], value_rows[head_ids, group_ids]])
    return stacked.reshape(2, ATT_TP * GROUPS * ROWS_G, HEAD_DIM).astype(jnp.bfloat16)


def draw_queries(key, part):
    device_count = ATT_TP * GROUPS
    drawn = jnp.clip(jax.random.normal(jax.random.fold_in(key, 7003), (device_count, GROUP_SEQS, TREE_ROWS, HEAD_SLICE), jnp.float32), -6.0, 6.0)
    return drawn.reshape(device_count * ROWS_G, HEAD_SLICE).astype(jnp.bfloat16)


def draw_kv_cache(key, part):
    base = jnp.clip(jax.random.normal(jax.random.fold_in(key, 7009), (2, KV_HEADS, GROUPS, POOL_DEV, PAGE_LEN, HEAD_DIM), jnp.float32), -6.0, 6.0)
    head_ids, group_ids = device_heads()
    spread = base[:, head_ids, group_ids]
    return spread.reshape(2, ATT_TP * GROUPS * POOL_DEV, PAGE_LEN, HEAD_DIM).astype(jnp.bfloat16)


def draw_block_table(key, part):
    group_keys = jax.random.split(jax.random.fold_in(key, 7005), GROUPS)
    orders = jax.vmap(lambda single: jax.random.permutation(single, POOL_DEV))(group_keys)
    tables = by_group(orders.reshape(GROUPS, GROUP_SEQS, PAGES_SEQ))
    return tables.reshape(ATT_TP * GROUPS * GROUP_SEQS, PAGES_SEQ).astype(jnp.int32)


def draw_cache_lengths(key, part):
    lengths = jax.random.randint(jax.random.fold_in(key, 7010), (GROUPS, GROUP_SEQS), 1, CACHE_MAX + 1, dtype=jnp.int32)
    longest = jax.random.randint(jax.random.fold_in(key, 7011), (GROUPS, 1), 0, GROUP_SEQS, dtype=jnp.int32)
    shortest = (longest + 1) % GROUP_SEQS
    seq_ids = jnp.arange(GROUP_SEQS, dtype=jnp.int32)[None, :]
    lengths = jnp.where(seq_ids == longest, CACHE_MAX, lengths)
    lengths = jnp.where(seq_ids == shortest, 1, lengths)
    return by_group(lengths).astype(jnp.int32)


def draw_parents(key, part):
    node_ids = jnp.arange(TREE_ROWS, dtype=jnp.int32)
    ceiling = jnp.broadcast_to(jnp.maximum(node_ids, 1), (GROUPS, GROUP_SEQS, TREE_ROWS))
    picked = jax.random.randint(jax.random.fold_in(key, 7006), (GROUPS, GROUP_SEQS, TREE_ROWS), 0, ceiling, dtype=jnp.int32)
    picked = jnp.where(node_ids == 0, -1, picked)
    return by_group(picked).reshape(ATT_TP * GROUPS * GROUP_SEQS, TREE_ROWS).astype(jnp.int32)


def draw_w_out(key, part):
    base = jnp.clip(jax.random.normal(jax.random.fold_in(key, 7012), (ATT_TP, HEAD_SLICE, D_MODEL), jnp.float32), -6.0, 6.0) * 256.0 ** (-0.5)
    slice_ids = jnp.arange(ATT_TP * GROUPS, dtype=jnp.int32) // GROUPS
    return base[slice_ids].reshape(ATT_TP * GROUPS * HEAD_SLICE, D_MODEL).astype(jnp.bfloat16)


def route_block(single, favored):
    spread = MOST_ROWS - MEAN_LOAD
    ranked = jax.random.permutation(jax.random.fold_in(single, 1), EXPERTS).astype(jnp.int32)
    ranked = jnp.where(ranked == favored, ranked[0], ranked).at[0].set(favored)
    offsets = jax.random.randint(jax.random.fold_in(single, 2), (EXPERTS // 2,), 0, spread + 1, dtype=jnp.int32)
    offsets = offsets.at[0].set(spread)
    quotas = jnp.stack([MEAN_LOAD + offsets, MEAN_LOAD - offsets], axis=1).reshape(EXPERTS)
    boundary = jnp.cumsum(quotas)
    ticket = jnp.arange(ROWS_DEV * TOP_K, dtype=jnp.int32)
    position = jnp.sum((ticket[:, None] >= boundary[None, :]).astype(jnp.int32), axis=1)
    layout = ranked[position].reshape(TOP_K, ROWS_DEV).T
    row_order = jax.random.permutation(jax.random.fold_in(single, 3), ROWS_DEV)
    layout = layout[row_order]
    rotation = jax.random.randint(jax.random.fold_in(single, 4), (ROWS_DEV, 1), 0, TOP_K, dtype=jnp.int32)
    columns = (jnp.arange(TOP_K, dtype=jnp.int32)[None, :] + rotation) % TOP_K
    return jnp.take_along_axis(layout, columns, axis=1)


def draw_expert_ids(key, part):
    device_count = TOKENS // ROWS_DEV
    favored = jax.random.randint(jax.random.fold_in(key, 7007), (), 0, EXPERTS, dtype=jnp.int32)
    device_keys = jax.random.split(jax.random.fold_in(key, 7008), device_count)
    layouts = jax.vmap(lambda single: route_block(single, favored))(device_keys)
    return layouts.reshape(TOKENS, TOP_K).astype(jnp.int32)


def block_scale(stream_key, dims, pieces, low, high):
    def one(dim, parts):
        steps = jax.random.uniform(jax.random.fold_in(jax.random.fold_in(stream_key, 6), dim), (parts,), jnp.float32, low / len(pieces), high / len(pieces))
        return jnp.repeat(jnp.exp(steps), dims[dim] // parts).reshape((-1,) + (1,) * (len(dims) - dim - 1))

    loudness = one(*pieces[0])
    for cut in pieces[1:]:
        loudness = loudness * one(*cut)
    return loudness


def normal_values(rng, dims, deviation, most, cuts=(), held_as=jnp.bfloat16):
    factor_of = block_scale(rng, dims, cuts, -0.22, 0.18) if cuts else 1.0
    entries = jax.random.normal(rng, dims, jnp.float32) * deviation * factor_of
    return jnp.minimum(jnp.maximum(entries, -most), most).astype(held_as)


def setup_inputs(seed: int = 0, part: int = 0) -> dict:
    key_of = jax.random.split(jax.random.key(seed), 13)
    part_keys = jax.random.split(jax.random.fold_in(key_of[12], part), 13)
    queries = draw_queries(jax.random.fold_in(jax.random.fold_in(key_of[12], part), 71), part)
    tree_kv = draw_tree_kv(jax.random.fold_in(jax.random.fold_in(key_of[12], part), 71), part)
    kv_cache = draw_kv_cache(jax.random.fold_in(jax.random.fold_in(key_of[12], part), 71), part)
    block_table = draw_block_table(jax.random.fold_in(jax.random.fold_in(key_of[12], part), 71), part)
    cache_lengths = draw_cache_lengths(jax.random.fold_in(jax.random.fold_in(key_of[12], part), 71), part)
    parents = draw_parents(jax.random.fold_in(jax.random.fold_in(key_of[12], part), 71), part)
    w_out = draw_w_out(jax.random.fold_in(key_of[12], 71), part)
    w_gate = normal_values(key_of[7], (EXPERTS, D_MODEL, FF_EXP), D_MODEL ** -0.5, 0.125, ((0, 16),))
    w_up = normal_values(key_of[8], (EXPERTS, D_MODEL, FF_EXP), D_MODEL ** -0.5, 0.125, ((0, 16),))
    w_down = normal_values(key_of[9], (EXPERTS, FF_EXP, D_MODEL), 192 ** -0.5, 0.4375, ((0, 16),))
    expert_ids = draw_expert_ids(jax.random.fold_in(jax.random.fold_in(key_of[12], part), 71), part)
    gate_weights = jnp.clip(jnp.exp(math.log(0.5) - 2.3025851 * jax.random.uniform(part_keys[11], (TOKENS, TOP_K), jnp.float32) ** block_scale(part_keys[11], (TOKENS, TOP_K), ((0, 16),), -0.2, 0.2)), 0.05, 0.5)
    return dict(queries=queries, tree_kv=tree_kv, kv_cache=kv_cache, block_table=block_table, cache_lengths=cache_lengths, parents=parents, w_out=w_out, w_gate=w_gate, w_up=w_up, w_down=w_down, expert_ids=expert_ids, gate_weights=gate_weights)


def ancestor_mask(parents):
    node_ids = jnp.broadcast_to(jnp.arange(TREE_ROWS, dtype=jnp.int32), parents.shape)
    columns = jnp.arange(TREE_ROWS, dtype=jnp.int32)
    reached = node_ids[:, :, None] == columns
    for repeat in range(TREE_ROWS):
        safe_ids = jnp.maximum(node_ids, 0).astype(jnp.int32)
        parent_of = jnp.take_along_axis(parents, safe_ids, axis=1).astype(jnp.int32)
        node_ids = jnp.where(node_ids >= 0, parent_of, -1).astype(jnp.int32)
        reached = reached | (node_ids[:, :, None] == columns)
    return reached


def attend_sequences(query_rows, own_keys, own_values, cache_keys, cache_values, lengths, parents):
    seq_count = parents.shape[0]
    cached = cache_keys.shape[1]
    query_heads = query_rows.reshape(seq_count, TREE_ROWS, QH_DEV, HEAD_DIM).astype(jnp.float32)
    key_rows = jnp.concatenate([cache_keys, own_keys], axis=1).astype(jnp.float32)
    value_rows = jnp.concatenate([cache_values, own_values], axis=1).astype(jnp.float32)
    scores = jnp.einsum('sqhd,skd->sqhk', query_heads, key_rows, precision=lax.Precision.HIGHEST) * (HEAD_DIM ** -0.5)
    positions = jnp.arange(cached, dtype=jnp.int32)
    cache_open = jnp.broadcast_to(positions[None, None, :] < lengths[:, None, None], (seq_count, TREE_ROWS, cached))
    allowed = jnp.concatenate([cache_open, ancestor_mask(parents)], axis=2)[:, :, None, :]
    masked = jnp.where(allowed, scores, -jnp.inf)
    highest = jnp.max(masked, axis=-1, keepdims=True)
    weights = jnp.exp(masked - highest)
    denominator = jnp.sum(weights, axis=-1, keepdims=True)
    rounded = lax.optimization_barrier(weights.astype(jnp.bfloat16)).astype(jnp.float32)
    blended = jnp.einsum('sqhk,skd->sqhd', rounded, value_rows, precision=lax.Precision.HIGHEST)
    return (blended / denominator).reshape(seq_count * TREE_ROWS, QH_DEV * HEAD_DIM).astype(jnp.bfloat16)


def reference(queries, tree_kv, kv_cache, block_table, cache_lengths, parents, w_out, w_gate, w_up, w_down, expert_ids, gate_weights):
    key_pool = kv_cache[0]
    value_pool = kv_cache[1]

    def one_device(summed, device):
        first_row = (device * ROWS_G).astype(jnp.int32)
        first_seq = (device * GROUP_SEQS).astype(jnp.int32)
        query_rows = lax.dynamic_slice_in_dim(queries, first_row, ROWS_G, 0)
        own_keys = lax.dynamic_slice_in_dim(tree_kv[0], first_row, ROWS_G, 0).reshape(GROUP_SEQS, TREE_ROWS, HEAD_DIM)
        own_values = lax.dynamic_slice_in_dim(tree_kv[1], first_row, ROWS_G, 0).reshape(GROUP_SEQS, TREE_ROWS, HEAD_DIM)
        pages = (lax.dynamic_slice_in_dim(block_table, first_seq, GROUP_SEQS, 0) + device * POOL_DEV).astype(jnp.int32)
        cache_keys = key_pool[pages].reshape(GROUP_SEQS, CACHE_MAX, HEAD_DIM)
        cache_values = value_pool[pages].reshape(GROUP_SEQS, CACHE_MAX, HEAD_DIM)
        lengths = lax.dynamic_slice_in_dim(cache_lengths, device.astype(jnp.int32), 1, 0).reshape(GROUP_SEQS)
        local_parents = lax.dynamic_slice_in_dim(parents, first_seq, GROUP_SEQS, 0)
        slice_rows = lax.dynamic_slice_in_dim(w_out, (device * HEAD_SLICE).astype(jnp.int32), HEAD_SLICE, 0)
        attended = attend_sequences(query_rows, own_keys, own_values, cache_keys, cache_values, lengths, local_parents)
        projected = jnp.dot(attended, slice_rows, preferred_element_type=jnp.float32)
        group_slot = (device % GROUPS).astype(jnp.int32)
        return summed.at[group_slot].add(projected), None

    initial = jnp.zeros((GROUPS, ROWS_G, D_MODEL), jnp.float32)
    summed, unused = lax.scan(one_device, initial, jnp.arange(N_WIDE, dtype=jnp.int32))
    hidden = summed.astype(jnp.bfloat16).reshape(GROUPS, ATT_TP, ROWS_DEV, D_MODEL)
    hidden = jnp.transpose(hidden, (1, 0, 2, 3)).reshape(TOKENS, D_MODEL)

    capacity = N_WIDE * MOST_ROWS
    row_numbers = jnp.arange(TOKENS, dtype=jnp.int32)

    def expert_step(running, packed):
        number, gate_matrix, up_matrix, down_matrix = packed
        matches = expert_ids == number
        chosen = jnp.any(matches, axis=1)
        row_weight = jnp.sum(jnp.where(matches, gate_weights, 0.0), axis=1)
        ranking = jnp.cumsum(chosen.astype(jnp.int32)) - 1
        target = jnp.where(chosen, ranking, capacity).astype(jnp.int32)
        picked = jnp.zeros((capacity,), jnp.int32).at[target].set(row_numbers, mode='drop')
        occupied = jnp.zeros((capacity,), jnp.float32).at[target].set(1.0, mode='drop')
        inputs = hidden[picked]
        gate_part = jnp.dot(inputs, gate_matrix, preferred_element_type=jnp.float32)
        up_part = jnp.dot(inputs, up_matrix, preferred_element_type=jnp.float32)
        activated = (jax.nn.silu(gate_part) * up_part).astype(jnp.bfloat16)
        produced = jnp.dot(activated, down_matrix, preferred_element_type=jnp.float32).astype(jnp.bfloat16)
        scaled = produced.astype(jnp.float32) * (row_weight[picked] * occupied)[:, None]
        return running.at[picked].add(scaled), None

    initial_rows = jnp.zeros((TOKENS, D_MODEL), jnp.float32)
    combined, unused_rows = lax.scan(expert_step, initial_rows, (jnp.arange(EXPERTS, dtype=jnp.int32), w_gate, w_up, w_down))
    return combined.astype(jnp.bfloat16)
```

```python
import functools

import jax
import jax.numpy as jnp
from jax import lax
from jax.experimental import pallas as pl
from jax.experimental.pallas import tpu as pltpu
from jax.sharding import PartitionSpec as P

CHUNKS = 4
TILE = 256
LANES = 128
MESH = pl.DeviceIdType.MESH


def layout(count, slices):
    bits = list(range(count.bit_length() - 1))
    shift = len(bits) - (slices.bit_length() - 1)
    far, near = bits[-1:], bits[shift:-1]
    groups = [tuple(far), tuple(near)]
    low = bits[1:shift]
    while low:
        groups.append(tuple(low[-2:]))
        low = low[:-2]
    if shift > 0:
        groups.append((0,))
    groups = [group for group in groups if group]
    starts = [0]
    for group in groups:
        starts.append(starts[-1] + len(group))
    return groups, starts, shift


def farthest_first(size):
    return sorted(range(1, 1 << size), key=lambda p: (-bin(p).count("1"), p))


def layer_kernel(
    count,
    block_table_in,
    cache_lengths_in,
    queries_in,
    tree_in,
    cache_in,
    parents_in,
    w_out_in,
    w_gate_in,
    w_up_in,
    w_down_in,
    expert_ids_in,
    gate_weights_in,
    out,
    block_table,
    cache_lengths,
    parents,
    expert_ids,
    gate_weights,
    queries,
    tree,
    cache,
    w_out,
    w_gate,
    w_up,
    w_down,
    attended,
    partial,
    hidden,
    routing,
    row_weight,
    gate_sum,
    up_sum,
    activated,
    produced,
    send_one,
    recv_one,
    send_two,
    recv_two,
    load_sem,
    one_send_sem,
    one_recv_sem,
    all_send_sem,
    all_recv_sem,
    route_send_sem,
    route_recv_sem,
    two_send_sem,
    two_recv_sem,
):
    me = lax.axis_index("wide")
    rows = out.shape[0]
    slices = attended.shape[0]
    groups, starts, slice_shift = layout(count, slices)
    bit_count = starts[-1]
    mine = [(me // (1 << bit)) % 2 for bit in range(bit_count)]

    def peer(group, pattern):
        device = me
        for number, bit in enumerate(group):
            if pattern >> number & 1:
                device = device + (1 - 2 * mine[bit]) * (1 << bit)
        return device

    barrier = pltpu.get_barrier_semaphore()
    friends = 0
    for group in groups:
        for pattern in range(1, 1 << len(group)):
            pl.semaphore_signal(
                barrier, inc=1, device_id={"wide": peer(group, pattern)}, device_id_type=MESH
            )
            friends += 1

    loads = []
    for number, (source, target) in enumerate(
        (
            (parents_in, parents),
            (queries_in, queries),
            (tree_in, tree),
            (cache_in, cache),
            (block_table_in, block_table),
            (cache_lengths_in, cache_lengths),
            (expert_ids_in, expert_ids),
            (gate_weights_in, gate_weights),
            (w_out_in, w_out),
            (w_gate_in.at[0], w_gate),
            (w_up_in.at[0], w_up),
            (w_down_in.at[0], w_down),
        )
    ):
        copy = pltpu.make_async_copy(source, target, load_sem.at[number])
        if number < 9:
            copy.start()
        loads.append(copy)

    seq_count, node_count = parents.shape
    head_dim = tree.shape[2]
    head_count = queries.shape[1] // head_dim
    page_count = block_table.shape[1]
    node_rows = lax.broadcasted_iota(jnp.int32, (node_count, node_count), 0)
    node_cols = lax.broadcasted_iota(jnp.int32, (node_count, node_count), 1)
    loads[0].wait()
    closures = []
    for seq in range(seq_count):
        linked = ((parents[seq : seq + 1, :] == node_rows) | (node_rows == node_cols)).astype(
            jnp.float32
        )
        closures.append(linked)
    for repeat in range(max(node_count - 1, 1).bit_length()):
        narrow = [linked.astype(jnp.bfloat16) for linked in closures]
        closures = [
            jnp.minimum(jnp.dot(linked, linked, preferred_element_type=jnp.float32), 1.0)
            for linked in narrow
        ]

    def relative_slice(place):
        index = 0
        for group, start in zip(groups, starts):
            for number, bit in enumerate(group):
                if bit >= slice_shift:
                    fixed = place >> (bit - slice_shift) & 1
                    index = index + (1 - mine[bit] if fixed else mine[bit]) * (
                        1 << (start + number)
                    )
        return index

    for copy in loads[1:6]:
        copy.wait()
    cached = page_count * cache.shape[2]
    positions = lax.broadcasted_iota(jnp.int32, (head_count * node_count, cached), 1)
    across = (((1,), (1,)), ((), ()))
    for seq in range(seq_count):
        first = seq * node_count
        last = first + node_count
        stacked = jnp.concatenate(
            [
                queries[first:last, head * head_dim : (head + 1) * head_dim]
                for head in range(head_count)
            ],
            axis=0,
        )
        pages = [block_table[seq, page] for page in range(page_count)]
        keys = jnp.concatenate([cache[0, page] for page in pages], axis=0)
        values = jnp.concatenate([cache[1, page] for page in pages], axis=0)
        scale = head_dim ** (-0.5)
        cache_scores = (
            lax.dot_general(stacked, keys, across, preferred_element_type=jnp.float32) * scale
        )
        tree_scores = (
            lax.dot_general(
                stacked, tree[0, first:last], across, preferred_element_type=jnp.float32
            )
            * scale
        )
        seen = jnp.concatenate([closures[seq].T] * head_count, axis=0) > 0.5
        cache_scores = jnp.where(positions < cache_lengths[0, seq], cache_scores, -jnp.inf)
        tree_scores = jnp.where(seen, tree_scores, -jnp.inf)
        highest = jnp.maximum(
            jnp.max(cache_scores, axis=1, keepdims=True),
            jnp.max(tree_scores, axis=1, keepdims=True),
        )
        cache_probs = jnp.exp(cache_scores - highest)
        tree_probs = jnp.exp(tree_scores - highest)
        denominator = jnp.sum(cache_probs, axis=1, keepdims=True) + jnp.sum(
            tree_probs, axis=1, keepdims=True
        )
        blended = jnp.dot(
            cache_probs.astype(jnp.bfloat16), values, preferred_element_type=jnp.float32
        ) + jnp.dot(
            tree_probs.astype(jnp.bfloat16),
            tree[1, first:last],
            preferred_element_type=jnp.float32,
        )
        blended = (blended / denominator).astype(jnp.bfloat16)
        for part in range(node_count // rows):
            index = relative_slice((first + part * rows) // rows)
            for head in range(head_count):
                top = head * node_count + part * rows
                attended[index, :, head * head_dim : (head + 1) * head_dim] = blended[
                    top : top + rows
                ]

    started = []

    def send(source, target, send_sem, recv_sem, device):
        copy = pltpu.make_async_remote_copy(
            src_ref=source,
            dst_ref=target,
            send_sem=send_sem,
            recv_sem=recv_sem,
            device_id={"wide": device},
            device_id_type=MESH,
        )
        copy.start()
        started.append(copy)
        return copy

    width = w_out.shape[1] // CHUNKS
    spans = [slice(chunk * width, (chunk + 1) * width) for chunk in range(CHUNKS)]

    class Gather:
        def __init__(self, buffer, send_sems, recv_sems):
            self.buffer = buffer
            self.send_sems = send_sems
            self.recv_sems = recv_sems
            self.copies = {}

        def start(self, step):
            held = 1 << starts[step]
            number = sum((1 << len(group)) - 1 for group in groups[:step])
            copies = []
            for pattern in farthest_first(len(groups[step])):
                slot = number + pattern - 1
                copies.append(
                    send(
                        self.buffer.at[pl.ds(0, held)],
                        self.buffer.at[pl.ds(pattern * held, held)],
                        self.send_sems.at[slot],
                        self.recv_sems.at[slot],
                        peer(groups[step], pattern),
                    )
                )
            self.copies[step] = copies

        def finish(self, step):
            for copy in self.copies[step]:
                copy.wait_recv()

    class Scatter:
        def __init__(self, kept, out_buffer, in_buffer, send_sems, recv_sems, steps):
            self.kept = kept
            self.out_buffer = out_buffer
            self.in_buffer = in_buffer
            self.send_sems = send_sems
            self.recv_sems = recv_sems
            self.steps = steps
            self.copies = {}
            self.first = {}
            self.number = {}
            first = number = 0
            for step in steps:
                self.first[step] = first
                self.number[step] = number
                first += (1 << starts[step + 1]) - (1 << starts[step])
                number += (1 << len(groups[step])) - 1

        def slot(self, step, place):
            return self.first[step] + place - (1 << starts[step])

        def launch(self, chunk, step, pattern):
            held = 1 << starts[step]
            region = pl.ds(self.slot(step, pattern * held), held)
            number = self.number[step] + pattern - 1
            self.copies.setdefault((chunk, step), []).append(
                send(
                    self.out_buffer.at[chunk, region],
                    self.in_buffer.at[chunk, region],
                    self.send_sems.at[chunk, number],
                    self.recv_sems.at[chunk, number],
                    peer(groups[step], pattern),
                )
            )

        def start(self, chunk, step, value):
            held = 1 << starts[step]
            for pattern in farthest_first(len(groups[step])):
                for place in range(pattern * held, (pattern + 1) * held):
                    self.out_buffer[chunk, self.slot(step, place)] = value(place).astype(
                        jnp.bfloat16
                    )
                self.launch(chunk, step, pattern)
            for place in range(held):
                self.kept[place, :, spans[chunk]] = value(place)

        def finish(self, chunk, step):
            for copy in self.copies[chunk, step]:
                copy.wait_recv()

        def value(self, chunk, step, place):
            total = self.kept[place, :, spans[chunk]]
            held = 1 << starts[step]
            for pattern in range(1, 1 << len(groups[step])):
                total = total + self.in_buffer[
                    chunk, self.slot(step, pattern * held + place)
                ].astype(jnp.float32)
            return total

    far_step, near_step, last_step = 0, 1, len(groups) - 1
    first_sum = Scatter(partial, send_one, recv_one, one_send_sem, one_recv_sem, [near_step])
    second_sum = Scatter(
        produced, send_two, recv_two, two_send_sem, two_recv_sem,
        list(range(last_step, -1, -1)),
    )
    gathers = [
        Gather(hidden.at[chunk], all_send_sem.at[chunk], all_recv_sem.at[chunk])
        for chunk in range(CHUNKS)
    ]
    route = Gather(routing, route_send_sem, route_recv_sem)

    loads[6].wait()
    loads[7].wait()
    ids = expert_ids[...].T
    weights_of = gate_weights[...].T
    lane_ids = lax.broadcasted_iota(jnp.int32, (rows, routing.shape[2]), 1)
    listed = jnp.zeros((rows, routing.shape[2]), jnp.float32)
    for k in range(expert_ids.shape[0]):
        listed += jnp.where(ids[:, k : k + 1] == lane_ids, weights_of[:, k : k + 1], 0.0)
    routing[0] = listed

    loads[8].wait()
    for copy in loads[9:]:
        copy.start()
    for chunk in range(CHUNKS):
        projected = jnp.dot(
            attended[...].reshape(slices * rows, attended.shape[2]),
            w_out[:, spans[chunk]],
            preferred_element_type=jnp.float32,
        )
        if chunk == 0:
            pl.semaphore_wait(barrier, friends)
        first_sum.start(
            chunk, near_step, lambda place: projected[place * rows : (place + 1) * rows]
        )
    route.start(far_step)

    held = 1 << starts[near_step]
    far_base = (slices - held)
    far_copies = {}
    far_sem = (1 << len(groups[near_step])) - 1
    for chunk in range(CHUNKS):
        first_sum.finish(chunk, near_step)
        for place in range(held):
            value = first_sum.value(chunk, near_step, place)
            partial[place, :, spans[chunk]] = value
            send_one[chunk, far_base + held - 1 - place] = value.astype(jnp.bfloat16)
        region = pl.ds(far_base, held)
        far_copies[chunk] = send(
            send_one.at[chunk, region],
            recv_one.at[chunk, region],
            one_send_sem.at[chunk, far_sem],
            one_recv_sem.at[chunk, far_sem],
            peer(groups[far_step], 1),
        )
    route.finish(far_step)
    route.start(near_step)
    for chunk in range(CHUNKS):
        far_copies[chunk].wait_recv()
        for place in range(held):
            hidden[chunk, place] = (
                partial[place, :, spans[chunk]]
                + recv_one[chunk, far_base + place].astype(jnp.float32)
            ).astype(jnp.bfloat16)
        gathers[chunk].start(near_step)

    for step in range(near_step, last_step):
        route.finish(step)
        route.start(step + 1)
        if step + 1 < last_step:
            for chunk in range(CHUNKS):
                gathers[chunk].finish(step)
                gathers[chunk].start(step + 1)

    hidden_width = w_gate.shape[1]
    tiles, tile_rows = activated.shape[:2]
    tile_blocks = tile_rows // rows
    joined = max(1, min(TILE // tile_rows, tiles))
    cuts = [
        slice(start, min(start + TILE, hidden_width)) for start in range(0, hidden_width, TILE)
    ]

    def over(total, step):
        if total == 1:
            step(0)
        else:
            pl.loop(0, total)(step)

    def accumulate_chunk(chunk):
        def accumulate(group):
            blocks = tile_blocks * joined
            taken = hidden[chunk, pl.ds(group * blocks, blocks)].reshape(
                blocks * rows, width
            )
            for cut in cuts:
                for sums, weights in ((gate_sum, w_gate), (up_sum, w_up)):
                    part = jnp.dot(
                        taken, weights[spans[chunk], cut], preferred_element_type=jnp.float32
                    )
                    for number in range(joined):
                        piece = part[number * tile_rows : (number + 1) * tile_rows]
                        if chunk == 0:
                            sums[group * joined + number, :, cut] = piece
                        else:
                            sums[group * joined + number, :, cut] += piece

        over(tiles // joined, accumulate)

    for chunk in range(CHUNKS):
        if last_step > near_step:
            gathers[chunk].finish(last_step - 1)
            gathers[chunk].start(last_step)
        if chunk == 0:
            loads[9].wait()
            loads[10].wait()
        else:
            gathers[chunk - 1].finish(last_step)
            accumulate_chunk(chunk - 1)
    route.finish(last_step)

    def weigh(tile):
        table = routing[pl.ds(tile * tile_blocks, tile_blocks)].reshape(
            tile_rows, routing.shape[2]
        )
        experts = lax.broadcasted_iota(jnp.int32, table.shape, 1)
        weight = jnp.sum(jnp.where(experts == me, table, 0.0), axis=1, keepdims=True)
        row_weight[tile] = jnp.broadcast_to(weight, (tile_rows, LANES))

    over(tiles, weigh)
    gathers[CHUNKS - 1].finish(last_step)
    accumulate_chunk(CHUNKS - 1)

    def activate(tile):
        for cut in cuts:
            gate = gate_sum[tile, :, cut]
            activated[tile, :, cut] = (
                gate / (1.0 + jnp.exp(-gate)) * up_sum[tile, :, cut]
            ).astype(jnp.bfloat16)

    over(tiles, activate)
    loads[11].wait()

    def down(chunk, tile):
        made = jnp.dot(
            activated[tile], w_down[:, spans[chunk]], preferred_element_type=jnp.float32
        )
        weight = jnp.concatenate([row_weight[tile]] * (width // LANES), axis=1)
        return (made * weight).reshape(tile_blocks, rows, width)

    half = tiles // 2
    for chunk in range(CHUNKS):

        def give(tile, chunk=chunk):
            first = second_sum.slot(last_step, (1 << starts[last_step])) + tile * tile_blocks
            send_two[chunk, pl.ds(first, tile_blocks)] = down(chunk, half + tile).astype(
                jnp.bfloat16
            )

        over(half, give)
        second_sum.launch(chunk, last_step, 1)
    for chunk in range(CHUNKS):

        def keep(tile, chunk=chunk):
            produced[pl.ds(tile * tile_blocks, tile_blocks), :, spans[chunk]] = down(chunk, tile)

        over(half, keep)
    for step in second_sum.steps:
        for chunk in range(CHUNKS):
            second_sum.finish(chunk, step)
            if step > 0:
                second_sum.start(
                    chunk, step - 1, functools.partial(second_sum.value, chunk, step)
                )
            else:
                out[:, spans[chunk]] = second_sum.value(chunk, step, 0).astype(jnp.bfloat16)
    for copy in started:
        copy.wait_send()


def body(
    queries,
    tree_kv,
    kv_cache,
    block_table,
    cache_lengths,
    parents,
    w_out,
    w_gate,
    w_up,
    w_down,
    expert_ids,
    gate_weights,
):
    count = lax.axis_size("wide")
    rows = expert_ids.shape[0]
    features = w_out.shape[1]
    hidden_width = w_gate.shape[2]
    slices = queries.shape[0] // rows
    groups, starts, slice_shift = layout(count, slices)
    width = features // CHUNKS
    lanes = -(-count // LANES) * LANES
    half_rows = count * rows // 2
    tile_rows = min(TILE, half_rows)
    tiles = count * rows // tile_rows
    links = sum((1 << len(group)) - 1 for group in groups)
    near = (1 << len(groups[1])) - 1
    hbm = pl.BlockSpec(memory_space=pl.ANY)
    vmem = pl.BlockSpec(memory_space=pltpu.VMEM)
    dma = pltpu.SemaphoreType.DMA
    ids, weights_of = expert_ids.T, gate_weights.T
    return pl.pallas_call(
        functools.partial(layer_kernel, count),
        out_shape=pltpu.VMEM((rows, features), jnp.bfloat16),
        in_specs=[hbm] * 12,
        out_specs=vmem,
        scratch_shapes=[
            pltpu.SMEM(block_table.shape, block_table.dtype),
            pltpu.SMEM(cache_lengths.shape, cache_lengths.dtype),
            pltpu.VMEM(parents.shape, parents.dtype),
            pltpu.VMEM(ids.shape, ids.dtype),
            pltpu.VMEM(weights_of.shape, weights_of.dtype),
            pltpu.VMEM(queries.shape, queries.dtype),
            pltpu.VMEM(tree_kv.shape, tree_kv.dtype),
            pltpu.VMEM(kv_cache.shape, kv_cache.dtype),
            pltpu.VMEM(w_out.shape, w_out.dtype),
            pltpu.VMEM(w_gate.shape[1:], w_gate.dtype),
            pltpu.VMEM(w_up.shape[1:], w_up.dtype),
            pltpu.VMEM(w_down.shape[1:], w_down.dtype),
            pltpu.VMEM((slices, rows, queries.shape[1]), jnp.bfloat16),
            pltpu.VMEM((1 << starts[1], rows, features), jnp.float32),
            pltpu.VMEM((CHUNKS, count, rows, width), jnp.bfloat16),
            pltpu.VMEM((count, rows, lanes), jnp.float32),
            pltpu.VMEM((tiles, tile_rows, LANES), jnp.float32),
            pltpu.VMEM((tiles, tile_rows, hidden_width), jnp.float32),
            pltpu.VMEM((tiles, tile_rows, hidden_width), jnp.float32),
            pltpu.VMEM((tiles, tile_rows, hidden_width), jnp.bfloat16),
            pltpu.VMEM((count // 2, rows, features), jnp.float32),
            pltpu.VMEM((CHUNKS, slices, rows, width), jnp.bfloat16),
            pltpu.VMEM((CHUNKS, slices, rows, width), jnp.bfloat16),
            pltpu.VMEM((CHUNKS, count - 1, rows, width), jnp.bfloat16),
            pltpu.VMEM((CHUNKS, count - 1, rows, width), jnp.bfloat16),
            dma((12,)),
            dma((CHUNKS, near + 1)),
            dma((CHUNKS, near + 1)),
            dma((CHUNKS, links)),
            dma((CHUNKS, links)),
            dma((links,)),
            dma((links,)),
            dma((CHUNKS, links)),
            dma((CHUNKS, links)),
        ],
        compiler_params=pltpu.CompilerParams(
            collective_id=0, has_side_effects=True, vmem_limit_bytes=60 << 20
        ),
    )(
        block_table,
        cache_lengths,
        queries,
        tree_kv,
        kv_cache,
        parents,
        w_out,
        w_gate,
        w_up,
        w_down,
        ids,
        weights_of,
    )


def solution(mesh):
    placed = (
        P(("groups", "wide"), None),
        P(None, ("groups", "wide"), None),
        P(None, ("groups", "wide"), None, None),
        P(("groups", "wide"), None),
        P(("groups", "wide"), None),
        P(("groups", "wide"), None),
        P("wide", None),
        P("wide", None, None),
        P("wide", None, None),
        P("wide", None, None),
        P(("groups", "wide"), None),
        P(("groups", "wide"), None),
    )
    return jax.shard_map(
        body, mesh=mesh, in_specs=placed, out_specs=P(("groups", "wide"), None), check_vma=False
    )
```

```python
import functools

import jax
import jax.numpy as jnp
from jax import lax
from jax.experimental import pallas as pl
from jax.experimental.pallas import tpu as pltpu
from jax.sharding import PartitionSpec as P

CHUNKS = 4
DIRECT = 2
TILE = 256
LANES = 128
MESH = pl.DeviceIdType.MESH


def layout(count, slices):
    bits = list(range(count.bit_length() - 1))
    shift = len(bits) - (slices.bit_length() - 1)
    far, near = bits[-1:], bits[shift:-1]
    groups = [tuple(far), tuple(near)]
    low = bits[1:shift]
    while low:
        groups.append(tuple(low[-2:]))
        low = low[:-2]
    groups = [group for group in groups if group]
    starts = [0]
    for group in groups:
        starts.append(starts[-1] + len(group))
    return groups, starts, shift


def second_plans(starts):
    plan = list(zip(starts, starts[1:]))[::-1]
    short = [(0, starts[-1])] if len(starts) == 3 else plan
    return [short if chunk >= CHUNKS - DIRECT else plan for chunk in range(CHUNKS)]


def farthest_first(low, high):
    patterns = range(1, 1 << (high - low))
    return [p << low for p in sorted(patterns, key=lambda p: (-bin(p).count("1"), p))]


def layer_kernel(
    count,
    block_table_in,
    cache_lengths_in,
    queries_in,
    tree_in,
    cache_in,
    parents_in,
    w_out_in,
    w_gate_in,
    w_up_in,
    w_down_in,
    expert_ids_in,
    gate_weights_in,
    out,
    block_table,
    cache_lengths,
    parents,
    expert_ids,
    gate_weights,
    queries,
    tree,
    cache,
    w_out,
    w_gate,
    w_up,
    w_down,
    attended,
    partial,
    hidden,
    routing,
    row_weight,
    gate_sum,
    up_sum,
    activated,
    produced,
    send_one,
    recv_one,
    send_two,
    recv_two,
    load_sem,
    send_sem,
    one_recv_sem,
    all_recv_sem,
    route_recv_sem,
    two_recv_sem,
    twin_send_sem,
    twin_recv_sem,
):
    me = lax.axis_index("wide")
    rows = out.shape[0]
    slices = attended.shape[0]
    groups, starts, slice_shift = layout(count, slices)
    places = 1 << starts[-1]
    mine = [(me // (1 << bit)) % 2 for bit in range(starts[-1] + 1)]
    twin = me + 1 - 2 * mine[0]

    order = [bit for group in groups for bit in group]

    def peer(place):
        device = me
        for number, bit in enumerate(order):
            if place >> number & 1:
                device = device + (1 - 2 * mine[bit]) * (1 << bit)
        return device

    rounds = list(zip(starts, starts[1:]))
    plans = second_plans(starts)
    friends = sorted(
        {
            pattern << low
            for low, high in sum(plans, rounds)
            for pattern in range(1, 1 << (high - low))
        }
    )
    friends = [twin] + [peer(place) for place in friends]
    barrier = pltpu.get_barrier_semaphore()
    for friend in friends:
        pl.semaphore_signal(barrier, inc=1, device_id={"wide": friend}, device_id_type=MESH)

    loads = []
    for number, (source, target) in enumerate(
        (
            (parents_in, parents),
            (queries_in, queries),
            (tree_in, tree),
            (cache_in, cache),
            (block_table_in, block_table),
            (cache_lengths_in, cache_lengths),
            (expert_ids_in, expert_ids),
            (gate_weights_in, gate_weights),
            (w_out_in, w_out),
            (w_gate_in.at[0], w_gate.at[0]),
            (w_up_in.at[0], w_up.at[0]),
            (w_down_in.at[0], w_down.at[0]),
        )
    ):
        copy = pltpu.make_async_copy(source, target, load_sem.at[number])
        if number < 9:
            copy.start()
        loads.append(copy)

    seq_count, node_count = parents.shape
    head_dim = tree.shape[2]
    head_count = queries.shape[1] // head_dim
    page_count = block_table.shape[1]
    node_rows = lax.broadcasted_iota(jnp.int32, (node_count, node_count), 0)
    node_cols = lax.broadcasted_iota(jnp.int32, (node_count, node_count), 1)
    loads[0].wait()
    closures = []
    for seq in range(seq_count):
        linked = ((parents[seq : seq + 1, :] == node_rows) | (node_rows == node_cols)).astype(
            jnp.float32
        )
        closures.append(linked)
    for repeat in range(max(node_count - 1, 1).bit_length()):
        narrow = [linked.astype(jnp.bfloat16) for linked in closures]
        closures = [
            jnp.minimum(jnp.dot(linked, linked, preferred_element_type=jnp.float32), 1.0)
            for linked in narrow
        ]

    def relative_slice(place):
        index = 0
        for group, start in zip(groups, starts):
            for number, bit in enumerate(group):
                if bit >= slice_shift:
                    fixed = place >> (bit - slice_shift) & 1
                    index = index + (1 - mine[bit] if fixed else mine[bit]) * (
                        1 << (start + number)
                    )
        return index

    for copy in loads[1:6]:
        copy.wait()
    cached = page_count * cache.shape[2]
    positions = lax.broadcasted_iota(jnp.int32, (head_count * node_count, cached), 1)
    across = (((1,), (1,)), ((), ()))
    for seq in range(seq_count):
        first = seq * node_count
        last = first + node_count
        stacked = jnp.concatenate(
            [
                queries[first:last, head * head_dim : (head + 1) * head_dim]
                for head in range(head_count)
            ],
            axis=0,
        )
        pages = [block_table[seq, page] for page in range(page_count)]
        keys = jnp.concatenate([cache[0, page] for page in pages], axis=0)
        values = jnp.concatenate([cache[1, page] for page in pages], axis=0)
        scale = head_dim ** (-0.5)
        cache_scores = (
            lax.dot_general(stacked, keys, across, preferred_element_type=jnp.float32) * scale
        )
        tree_scores = (
            lax.dot_general(
                stacked, tree[0, first:last], across, preferred_element_type=jnp.float32
            )
            * scale
        )
        seen = jnp.concatenate([closures[seq].T] * head_count, axis=0) > 0.5
        cache_scores = jnp.where(positions < cache_lengths[0, seq], cache_scores, -jnp.inf)
        tree_scores = jnp.where(seen, tree_scores, -jnp.inf)
        highest = jnp.maximum(
            jnp.max(cache_scores, axis=1, keepdims=True),
            jnp.max(tree_scores, axis=1, keepdims=True),
        )
        cache_probs = jnp.exp(cache_scores - highest)
        tree_probs = jnp.exp(tree_scores - highest)
        denominator = jnp.sum(cache_probs, axis=1, keepdims=True) + jnp.sum(
            tree_probs, axis=1, keepdims=True
        )
        blended = jnp.dot(
            cache_probs.astype(jnp.bfloat16), values, preferred_element_type=jnp.float32
        ) + jnp.dot(
            tree_probs.astype(jnp.bfloat16),
            tree[1, first:last],
            preferred_element_type=jnp.float32,
        )
        blended = (blended / denominator).astype(jnp.bfloat16)
        for part in range(node_count // rows):
            index = relative_slice((first + part * rows) // rows)
            for head in range(head_count):
                top = head * node_count + part * rows
                attended[index, :, head * head_dim : (head + 1) * head_dim] = blended[
                    top : top + rows
                ]

    def send(source, target, send_sem, recv_sem, device):
        pltpu.make_async_remote_copy(
            src_ref=source,
            dst_ref=target,
            send_sem=send_sem,
            recv_sem=recv_sem,
            device_id={"wide": device},
            device_id_type=MESH,
        ).start()

    def await_bytes(view, sem):
        pltpu.make_async_copy(view, view, sem).wait()

    width = w_out.shape[1] // CHUNKS
    spans = [slice(chunk * width, (chunk + 1) * width) for chunk in range(CHUNKS)]

    class Gather:
        def __init__(self, buffer, send_sem, recv_sems):
            self.buffer = buffer
            self.send_sem = send_sem
            self.recv_sems = recv_sems

        def start(self, step):
            held = 1 << starts[step]
            for place in farthest_first(*rounds[step]):
                send(
                    self.buffer.at[pl.ds(0, held)],
                    self.buffer.at[pl.ds(place, held)],
                    self.send_sem,
                    self.recv_sems.at[step],
                    peer(place),
                )

        def finish(self, step):
            held = 1 << starts[step]
            region = pl.ds(held, (1 << starts[step + 1]) - held)
            await_bytes(self.buffer.at[region], self.recv_sems.at[step])

    class Scatter:
        def __init__(self, kept, out_buffer, in_buffer, send_sem, recv_sems, plans):
            self.kept = kept
            self.out_buffer = out_buffer
            self.in_buffer = in_buffer
            self.send_sem = send_sem
            self.recv_sems = recv_sems
            self.plans = plans

        def slot(self, chunk, turn, place):
            plan = self.plans[chunk]
            first = sum((1 << high) - (1 << low) for low, high in plan[:turn])
            return first + place - (1 << plan[turn][0])

        def launch(self, chunk, turn, place):
            held = 1 << self.plans[chunk][turn][0]
            region = pl.ds(self.slot(chunk, turn, place), held)
            send(
                self.out_buffer.at[chunk, region],
                self.in_buffer.at[chunk, region],
                self.send_sem,
                self.recv_sems.at[chunk, turn],
                peer(place),
            )

        def start(self, chunk, turn, value):
            low, high = self.plans[chunk][turn]
            for first in farthest_first(low, high):
                for place in range(first, first + (1 << low)):
                    self.out_buffer[chunk, self.slot(chunk, turn, place)] = value(place).astype(
                        jnp.bfloat16
                    )
                self.launch(chunk, turn, first)
            for place in range(1 << low):
                self.kept[place, :, spans[chunk]] = value(place)

        def finish(self, chunk, turn):
            low, high = self.plans[chunk][turn]
            region = pl.ds(self.slot(chunk, turn, 1 << low), (1 << high) - (1 << low))
            await_bytes(self.in_buffer.at[chunk, region], self.recv_sems.at[chunk, turn])

        def value(self, chunk, turn, place):
            low, high = self.plans[chunk][turn]
            total = self.kept[place, :, spans[chunk]]
            for first in range(1 << low, 1 << high, 1 << low):
                total = total + self.in_buffer[
                    chunk, self.slot(chunk, turn, first + place)
                ].astype(jnp.float32)
            return total

    far_step, near_step, last_step = 0, 1, len(groups) - 1
    first_sum = Scatter(partial, send_one, recv_one, send_sem.at[0], one_recv_sem,
        [[rounds[near_step]]] * CHUNKS)
    second_sum = Scatter(
        produced, send_two, recv_two, send_sem.at[1], two_recv_sem,
        plans,
    )
    gathers = [
        Gather(hidden.at[chunk], send_sem.at[2], all_recv_sem.at[chunk])
        for chunk in range(CHUNKS)
    ]
    route = Gather(routing, send_sem.at[3], route_recv_sem)

    loads[8].wait()
    for copy in loads[9:]:
        copy.start()
    for chunk in range(CHUNKS):
        projected = jnp.dot(
            attended[...].reshape(slices * rows, attended.shape[2]),
            w_out[:, spans[chunk]],
            preferred_element_type=jnp.float32,
        )
        if chunk == 0:
            pl.semaphore_wait(barrier, len(friends))
        first_sum.start(
            chunk, 0, lambda place: projected[place * rows : (place + 1) * rows]
        )
    loads[6].wait()
    loads[7].wait()
    ids = expert_ids[...].T
    weights_of = gate_weights[...].T
    lane_ids = lax.broadcasted_iota(jnp.int32, (rows, routing.shape[2]), 1)
    listed = jnp.zeros((rows, routing.shape[2]), jnp.float32)
    for k in range(expert_ids.shape[0]):
        listed += jnp.where(ids[:, k : k + 1] == lane_ids, weights_of[:, k : k + 1], 0.0)
    routing[0] = listed

    route.start(far_step)
    for number, (source, target) in enumerate(
        ((w_gate_in, w_gate), (w_up_in, w_up), (w_down_in, w_down))
    ):
        send(source.at[0], target.at[1], twin_send_sem.at[number], twin_recv_sem.at[number], twin)

    held = 1 << starts[near_step]
    far_base = (slices - held)
    for chunk in range(CHUNKS):
        first_sum.finish(chunk, 0)
        for place in range(held):
            value = first_sum.value(chunk, 0, place)
            partial[place, :, spans[chunk]] = value
            send_one[chunk, far_base + held - 1 - place] = value.astype(jnp.bfloat16)
        region = pl.ds(far_base, held)
        send(
            send_one.at[chunk, region],
            recv_one.at[chunk, region],
            send_sem.at[0],
            one_recv_sem.at[chunk, 1],
            peer(1),
        )
    route.finish(far_step)
    route.start(near_step)
    for chunk in range(CHUNKS):
        await_bytes(
            recv_one.at[chunk, pl.ds(far_base, held)], one_recv_sem.at[chunk, 1]
        )
        for place in range(held):
            hidden[chunk, place] = (
                partial[place, :, spans[chunk]]
                + recv_one[chunk, far_base + place].astype(jnp.float32)
            ).astype(jnp.bfloat16)
        gathers[chunk].start(near_step)

    for step in range(near_step, last_step):
        route.finish(step)
        route.start(step + 1)
        if step + 1 < last_step:
            for chunk in range(CHUNKS):
                gathers[chunk].finish(step)
                gathers[chunk].start(step + 1)

    hidden_width = w_gate.shape[2]
    tiles, tile_rows = activated.shape[1:3]
    tile_blocks = tile_rows // rows
    cuts = [
        slice(start, min(start + TILE, hidden_width)) for start in range(0, hidden_width, TILE)
    ]

    def over_tiles(step):
        if tiles == 1:
            step(0)
        else:
            pl.loop(0, tiles)(step)

    def weigh(tile):
        table = routing[pl.ds(tile * tile_blocks, tile_blocks)].reshape(
            tile_rows, routing.shape[2]
        )
        experts = lax.broadcasted_iota(jnp.int32, table.shape, 1)
        for number, expert in enumerate((me, twin)):
            weight = jnp.sum(jnp.where(experts == expert, table, 0.0), axis=1, keepdims=True)
            row_weight[number, tile] = jnp.broadcast_to(weight, (tile_rows, LANES))

    for chunk in range(CHUNKS):
        gathers[chunk].finish(last_step)
        if chunk == 0:
            for number, weights in enumerate((w_gate, w_up)):
                loads[9 + number].wait()
                await_bytes(weights.at[1], twin_recv_sem.at[number])

        def accumulate(tile, chunk=chunk):
            taken = hidden[chunk, pl.ds(tile * tile_blocks, tile_blocks)].reshape(
                tile_rows, width
            )
            for number in range(2):
                for cut in cuts:
                    for sums, weights in ((gate_sum, w_gate), (up_sum, w_up)):
                        part = jnp.dot(
                            taken,
                            weights[number, spans[chunk], cut],
                            preferred_element_type=jnp.float32,
                        )
                        if chunk == 0:
                            sums[number, tile, :, cut] = part
                        else:
                            sums[number, tile, :, cut] += part

        over_tiles(accumulate)
        if chunk == 0:
            route.finish(last_step)
            over_tiles(weigh)

    def activate(tile):
        for number in range(2):
            for cut in cuts:
                gate = gate_sum[number, tile, :, cut]
                activated[number, tile, :, cut] = (
                    gate / (1.0 + jnp.exp(-gate)) * up_sum[number, tile, :, cut]
                ).astype(jnp.bfloat16)

    over_tiles(activate)
    loads[11].wait()
    await_bytes(w_down.at[1], twin_recv_sem.at[2])

    def down(chunk, tile):
        total = None
        for number in range(2):
            made = jnp.dot(
                activated[number, tile],
                w_down[number, :, spans[chunk]],
                preferred_element_type=jnp.float32,
            )
            weighed = made * jnp.concatenate(
                [row_weight[number, tile]] * (width // LANES), axis=1
            )
            total = weighed if total is None else total + weighed
        return total.reshape(tile_blocks, rows, width)

    for chunk in range(CHUNKS):
        made = [down(chunk, tile) for tile in range(tiles)]
        second_sum.start(
            chunk, 0, lambda place: made[place // tile_blocks][place % tile_blocks]
        )
    for turn in range(len(rounds)):
        for chunk in range(CHUNKS):
            turns = len(plans[chunk])
            if turn >= turns:
                continue
            second_sum.finish(chunk, turn)
            if turn + 1 < turns:
                second_sum.start(
                    chunk, turn + 1, functools.partial(second_sum.value, chunk, turn)
                )
            else:
                out[:, spans[chunk]] = second_sum.value(chunk, turn, 0).astype(jnp.bfloat16)
    await_bytes(send_one, send_sem.at[0])
    await_bytes(send_two, send_sem.at[1])
    given = sum(
        ((1 << len(groups[step])) - 1) << starts[step] for step in range(near_step, last_step + 1)
    )
    await_bytes(hidden.at[:, pl.ds(0, given)], send_sem.at[2])
    await_bytes(routing.at[pl.ds(1, places - 1)], send_sem.at[3])
    for number, weights in enumerate((w_gate, w_up, w_down)):
        await_bytes(weights.at[0], twin_send_sem.at[number])


def body(
    queries,
    tree_kv,
    kv_cache,
    block_table,
    cache_lengths,
    parents,
    w_out,
    w_gate,
    w_up,
    w_down,
    expert_ids,
    gate_weights,
):
    count = lax.axis_size("wide")
    rows = expert_ids.shape[0]
    features = w_out.shape[1]
    hidden_width = w_gate.shape[2]
    slices = queries.shape[0] // rows
    groups, starts, slice_shift = layout(count, slices)
    width = features // CHUNKS
    lanes = -(-count // LANES) * LANES
    places = 1 << starts[-1]
    tile_rows = min(TILE, places * rows)
    tiles = places * rows // tile_rows
    hbm = pl.BlockSpec(memory_space=pl.ANY)
    vmem = pl.BlockSpec(memory_space=pltpu.VMEM)
    dma = pltpu.SemaphoreType.DMA
    ids, weights_of = expert_ids.T, gate_weights.T
    return pl.pallas_call(
        functools.partial(layer_kernel, count),
        out_shape=pltpu.VMEM((rows, features), jnp.bfloat16),
        in_specs=[hbm] * 12,
        out_specs=vmem,
        scratch_shapes=[
            pltpu.SMEM(block_table.shape, block_table.dtype),
            pltpu.SMEM(cache_lengths.shape, cache_lengths.dtype),
            pltpu.VMEM(parents.shape, parents.dtype),
            pltpu.VMEM(ids.shape, ids.dtype),
            pltpu.VMEM(weights_of.shape, weights_of.dtype),
            pltpu.VMEM(queries.shape, queries.dtype),
            pltpu.VMEM(tree_kv.shape, tree_kv.dtype),
            pltpu.VMEM(kv_cache.shape, kv_cache.dtype),
            pltpu.VMEM(w_out.shape, w_out.dtype),
            pltpu.VMEM((2, *w_gate.shape[1:]), w_gate.dtype),
            pltpu.VMEM((2, *w_up.shape[1:]), w_up.dtype),
            pltpu.VMEM((2, *w_down.shape[1:]), w_down.dtype),
            pltpu.VMEM((slices, rows, queries.shape[1]), jnp.bfloat16),
            pltpu.VMEM((1 << starts[1], rows, features), jnp.float32),
            pltpu.VMEM((CHUNKS, places, rows, width), jnp.bfloat16),
            pltpu.VMEM((places, rows, lanes), jnp.float32),
            pltpu.VMEM((2, tiles, tile_rows, LANES), jnp.float32),
            pltpu.VMEM((2, tiles, tile_rows, hidden_width), jnp.float32),
            pltpu.VMEM((2, tiles, tile_rows, hidden_width), jnp.float32),
            pltpu.VMEM((2, tiles, tile_rows, hidden_width), jnp.bfloat16),
            pltpu.VMEM((1 << starts[-2], rows, features), jnp.float32),
            pltpu.VMEM((CHUNKS, slices, rows, width), jnp.bfloat16),
            pltpu.VMEM((CHUNKS, slices, rows, width), jnp.bfloat16),
            pltpu.VMEM((CHUNKS, places - 1, rows, width), jnp.bfloat16),
            pltpu.VMEM((CHUNKS, places - 1, rows, width), jnp.bfloat16),
            dma((12,)),
            dma((4,)),
            dma((CHUNKS, 2)),
            dma((CHUNKS, len(groups))),
            dma((len(groups),)),
            dma((CHUNKS, len(groups))),
            dma((3,)),
            dma((3,)),
        ],
        compiler_params=pltpu.CompilerParams(
            collective_id=0, has_side_effects=True, vmem_limit_bytes=60 << 20
        ),
    )(
        block_table,
        cache_lengths,
        queries,
        tree_kv,
        kv_cache,
        parents,
        w_out,
        w_gate,
        w_up,
        w_down,
        ids,
        weights_of,
    )


def solution(mesh):
    placed = (
        P(("groups", "wide"), None),
        P(None, ("groups", "wide"), None),
        P(None, ("groups", "wide"), None, None),
        P(("groups", "wide"), None),
        P(("groups", "wide"), None),
        P(("groups", "wide"), None),
        P("wide", None),
        P("wide", None, None),
        P("wide", None, None),
        P("wide", None, None),
        P(("groups", "wide"), None),
        P(("groups", "wide"), None),
    )
    return jax.shard_map(
        body, mesh=mesh, in_specs=placed, out_specs=P(("groups", "wide"), None), check_vma=False
    )
```

```python
import functools

import jax
import jax.numpy as jnp
from jax import lax
from jax.experimental import pallas as pl
from jax.experimental.pallas import tpu as pltpu
from jax.sharding import PartitionSpec as P

FRONT = (3, 5, 5, 3)
BACK = (4, 4, 4, 4)
DIRECT = 2
CHUNKS = len(FRONT)
TILE = 256
LANES = 128
MESH = pl.DeviceIdType.MESH


def layout(count, slices):
    bits = list(range(count.bit_length() - 1))
    shift = len(bits) - (slices.bit_length() - 1)
    far, near = bits[-1:], bits[shift:-1]
    groups = [tuple(far), tuple(near)]
    low = bits[1:shift]
    while low:
        groups.append(tuple(low[-2:]))
        low = low[:-2]
    groups = [group for group in groups if group]
    starts = [0]
    for group in groups:
        starts.append(starts[-1] + len(group))
    return groups, starts, shift


def second_plans(starts):
    plan = list(zip(starts, starts[1:]))[::-1]
    short = [(0, starts[-1])] if len(starts) == 3 else plan
    return [short if chunk >= len(BACK) - DIRECT else plan for chunk in range(len(BACK))]


def shares_of(features, shares):
    spans, start = [], 0
    for share in shares:
        stop = start + share * features // sum(shares)
        spans.append(slice(start, stop))
        start = stop
    return spans


def widest_of(features, shares):
    return max(span.stop - span.start for span in shares_of(features, shares))


def farthest_first(low, high):
    def distance(place):
        return (-(place & 1), -bin(place).count("1"), place)

    return sorted(range(1 << low, 1 << high, 1 << low), key=distance)


def layer_kernel(
    count,
    block_table_in,
    cache_lengths_in,
    queries_in,
    tree_in,
    cache_in,
    parents_in,
    w_out_in,
    w_gate_in,
    w_up_in,
    w_down_in,
    expert_ids_in,
    gate_weights_in,
    out,
    block_table,
    cache_lengths,
    parents,
    expert_ids,
    gate_weights,
    queries,
    tree,
    cache,
    w_out,
    w_gate,
    w_up,
    w_down,
    attended,
    partial,
    hidden,
    routing,
    row_weight,
    gate_sum,
    up_sum,
    activated,
    produced,
    send_one,
    recv_one,
    send_two,
    recv_two,
    load_sem,
    send_sem,
    one_recv_sem,
    all_recv_sem,
    route_recv_sem,
    two_recv_sem,
    twin_send_sem,
    twin_recv_sem,
):
    me = lax.axis_index("wide")
    rows = out.shape[0]
    slices = attended.shape[0]
    groups, starts, slice_shift = layout(count, slices)
    places = 1 << starts[-1]
    mine = [(me // (1 << bit)) % 2 for bit in range(starts[-1] + 1)]
    twin = me + 1 - 2 * mine[0]

    order = [bit for group in groups for bit in group]

    def peer(place):
        device = me
        for number, bit in enumerate(order):
            if place >> number & 1:
                device = device + (1 - 2 * mine[bit]) * (1 << bit)
        return device

    rounds = list(zip(starts, starts[1:]))
    plans = second_plans(starts)
    friends = sorted(
        {
            pattern << low
            for low, high in sum(plans, rounds)
            for pattern in range(1, 1 << (high - low))
        }
    )
    friends = [twin] + [peer(place) for place in friends]
    barrier = pltpu.get_barrier_semaphore()
    for friend in friends:
        pl.semaphore_signal(barrier, inc=1, device_id={"wide": friend}, device_id_type=MESH)

    loads = []
    for number, (source, target) in enumerate(
        (
            (parents_in, parents),
            (queries_in, queries),
            (tree_in, tree),
            (cache_in, cache),
            (block_table_in, block_table),
            (cache_lengths_in, cache_lengths),
            (expert_ids_in, expert_ids),
            (gate_weights_in, gate_weights),
            (w_gate_in.at[0], w_gate.at[0]),
            (w_up_in.at[0], w_up.at[0]),
            (w_down_in.at[0], w_down.at[0]),
        )
    ):
        copy = pltpu.make_async_copy(source, target, load_sem.at[number])
        if number < 6:
            copy.start()
        loads.append(copy)
    out_loads = []
    for number, span in enumerate(shares_of(w_out.shape[1], FRONT)):
        view = (slice(None), pl.ds(span.start, span.stop - span.start))
        out_loads.append(
            pltpu.make_async_copy(w_out_in.at[view], w_out.at[view], load_sem.at[11 + number])
        )

    seq_count, node_count = parents.shape
    head_dim = tree.shape[2]
    head_count = queries.shape[1] // head_dim
    page_count = block_table.shape[1]
    node_rows = lax.broadcasted_iota(jnp.int32, (node_count, node_count), 0)
    node_cols = lax.broadcasted_iota(jnp.int32, (node_count, node_count), 1)
    loads[0].wait()
    for copy in out_loads + loads[6:8]:
        copy.start()
    closures = []
    for seq in range(seq_count):
        linked = ((parents[seq : seq + 1, :] == node_rows) | (node_rows == node_cols)).astype(
            jnp.float32
        )
        closures.append(linked)
    for repeat in range(max(node_count - 1, 1).bit_length()):
        narrow = [linked.astype(jnp.bfloat16) for linked in closures]
        closures = [
            jnp.dot(linked, linked, preferred_element_type=jnp.float32) for linked in narrow
        ]

    def relative_slice(place):
        index = 0
        for group, start in zip(groups, starts):
            for number, bit in enumerate(group):
                if bit >= slice_shift:
                    fixed = place >> (bit - slice_shift) & 1
                    index = index + (1 - mine[bit] if fixed else mine[bit]) * (
                        1 << (start + number)
                    )
        return index

    def send(source, target, send_sem, recv_sem, device):
        pltpu.make_async_remote_copy(
            src_ref=source,
            dst_ref=target,
            send_sem=send_sem,
            recv_sem=recv_sem,
            device_id={"wide": device},
            device_id_type=MESH,
        ).start()

    def await_bytes(view, sem):
        pltpu.make_async_copy(view, view, sem).wait()

    shared = ((w_gate_in, w_gate), (w_up_in, w_up), (w_down_in, w_down))

    def share(number):
        source, target = shared[number]
        send(source.at[0], target.at[1], twin_send_sem.at[number], twin_recv_sem.at[number], twin)

    for copy in loads[1:6]:
        copy.wait()
    cached = page_count * cache.shape[2]
    positions = lax.broadcasted_iota(jnp.int32, (head_count * node_count, cached), 1)
    across = (((1,), (1,)), ((), ()))
    for seq in range(seq_count):
        first = seq * node_count
        last = first + node_count
        stacked = jnp.concatenate(
            [
                queries[first:last, head * head_dim : (head + 1) * head_dim]
                for head in range(head_count)
            ],
            axis=0,
        )
        pages = [block_table[seq, page] for page in range(page_count)]
        keys = jnp.concatenate([cache[0, page] for page in pages], axis=0)
        values = jnp.concatenate([cache[1, page] for page in pages], axis=0)
        scale = head_dim ** (-0.5)
        cache_scores = (
            lax.dot_general(stacked, keys, across, preferred_element_type=jnp.float32) * scale
        )
        tree_scores = (
            lax.dot_general(
                stacked, tree[0, first:last], across, preferred_element_type=jnp.float32
            )
            * scale
        )
        seen = jnp.concatenate([closures[seq].T] * head_count, axis=0) > 0.5
        cache_scores = jnp.where(positions < cache_lengths[0, seq], cache_scores, -jnp.inf)
        tree_scores = jnp.where(seen, tree_scores, -jnp.inf)
        highest = jnp.maximum(
            jnp.max(cache_scores, axis=1, keepdims=True),
            jnp.max(tree_scores, axis=1, keepdims=True),
        )
        cache_probs = jnp.exp(cache_scores - highest)
        tree_probs = jnp.exp(tree_scores - highest)
        denominator = jnp.sum(cache_probs, axis=1, keepdims=True) + jnp.sum(
            tree_probs, axis=1, keepdims=True
        )
        blended = jnp.dot(
            cache_probs.astype(jnp.bfloat16), values, preferred_element_type=jnp.float32
        ) + jnp.dot(
            tree_probs.astype(jnp.bfloat16),
            tree[1, first:last],
            preferred_element_type=jnp.float32,
        )
        blended = (blended / denominator).astype(jnp.bfloat16)
        for part in range(node_count // rows):
            index = relative_slice((first + part * rows) // rows)
            for head in range(head_count):
                top = head * node_count + part * rows
                attended[index, :, head * head_dim : (head + 1) * head_dim] = blended[
                    top : top + rows
                ]

    spans = shares_of(w_out.shape[1], FRONT)
    columns = [pl.ds(0, span.stop - span.start) for span in spans]
    back_spans = shares_of(w_out.shape[1], BACK)

    class Gather:
        def __init__(self, buffer, send_sem, recv_sems):
            self.buffer = buffer
            self.send_sem = send_sem
            self.recv_sems = recv_sems

        def start(self, step):
            held = 1 << starts[step]
            for place in farthest_first(*rounds[step]):
                send(
                    self.buffer.at[pl.ds(0, held)],
                    self.buffer.at[pl.ds(place, held)],
                    self.send_sem,
                    self.recv_sems.at[step],
                    peer(place),
                )

        def finish(self, step):
            held = 1 << starts[step]
            region = pl.ds(held, (1 << starts[step + 1]) - held)
            await_bytes(self.buffer.at[region], self.recv_sems.at[step])

    class Scatter:
        def __init__(self, kept, out_buffer, in_buffer, send_sem, recv_sems, plans, spans):
            self.spans = spans
            self.kept = kept
            self.out_buffer = out_buffer
            self.in_buffer = in_buffer
            self.send_sem = send_sem
            self.recv_sems = recv_sems
            self.plans = plans
            self.columns = [pl.ds(0, span.stop - span.start) for span in spans]

        def slot(self, chunk, turn, place):
            plan = self.plans[chunk]
            first = sum((1 << high) - (1 << low) for low, high in plan[:turn])
            return first + place - (1 << plan[turn][0])

        def launch(self, chunk, turn, place):
            held = 1 << self.plans[chunk][turn][0]
            region = pl.ds(self.slot(chunk, turn, place), held)
            send(
                self.out_buffer.at[chunk, region, :, self.columns[chunk]],
                self.in_buffer.at[chunk, region, :, self.columns[chunk]],
                self.send_sem,
                self.recv_sems.at[chunk, turn],
                peer(place),
            )

        def start(self, chunk, turn, value):
            low, high = self.plans[chunk][turn]
            for first in farthest_first(low, high):
                for place in range(first, first + (1 << low)):
                    self.out_buffer[
                        chunk, self.slot(chunk, turn, place), :, self.columns[chunk]
                    ] = value(place).astype(jnp.bfloat16)
                self.launch(chunk, turn, first)
            for place in range(1 << low):
                self.kept[place, :, self.spans[chunk]] = value(place)

        def finish(self, chunk, turn):
            low, high = self.plans[chunk][turn]
            region = pl.ds(self.slot(chunk, turn, 1 << low), (1 << high) - (1 << low))
            await_bytes(
                self.in_buffer.at[chunk, region, :, self.columns[chunk]],
                self.recv_sems.at[chunk, turn],
            )

        def value(self, chunk, turn, place):
            low, high = self.plans[chunk][turn]
            total = self.kept[place, :, self.spans[chunk]]
            for first in range(1 << low, 1 << high, 1 << low):
                total = total + self.in_buffer[
                    chunk, self.slot(chunk, turn, first + place), :, self.columns[chunk]
                ].astype(jnp.float32)
            return total

    far_step, near_step, last_step = 0, 1, len(groups) - 1
    first_sum = Scatter(partial, send_one, recv_one, send_sem.at[0], one_recv_sem,
        [[rounds[near_step]]] * CHUNKS, spans,
    )
    second_sum = Scatter(
        produced, send_two, recv_two, send_sem.at[1], two_recv_sem,
        plans, back_spans,
    )
    gathers = [
        Gather(hidden.at[chunk, :, :, columns[chunk]], send_sem.at[2], all_recv_sem.at[chunk])
        for chunk in range(CHUNKS)
    ]
    route = Gather(routing, send_sem.at[3], route_recv_sem)

    pl.semaphore_wait(barrier, len(friends))
    share(0)
    share(1)
    for chunk in range(CHUNKS):
        out_loads[chunk].wait()
        projected = jnp.dot(
            attended[...].reshape(slices * rows, attended.shape[2]),
            w_out[:, spans[chunk]],
            preferred_element_type=jnp.float32,
        )
        first_sum.start(
            chunk, 0, lambda place: projected[place * rows : (place + 1) * rows]
        )
    loads[6].wait()
    loads[7].wait()
    ids = expert_ids[...].T
    weights_of = gate_weights[...].T
    lane_ids = lax.broadcasted_iota(jnp.int32, (rows, routing.shape[2]), 1)
    listed = jnp.zeros((rows, routing.shape[2]), jnp.float32)
    for k in range(expert_ids.shape[0]):
        listed += jnp.where(ids[:, k : k + 1] == lane_ids, weights_of[:, k : k + 1], 0.0)
    routing[0] = listed

    route.start(far_step)
    for copy in loads[8:]:
        copy.start()

    held = 1 << starts[near_step]
    far_base = (slices - held)
    for chunk in range(CHUNKS):
        first_sum.finish(chunk, 0)
        for place in range(held):
            value = first_sum.value(chunk, 0, place)
            partial[place, :, spans[chunk]] = value
            send_one[chunk, far_base + held - 1 - place, :, columns[chunk]] = value.astype(
                jnp.bfloat16
            )
        region = pl.ds(far_base, held)
        send(
            send_one.at[chunk, region, :, columns[chunk]],
            recv_one.at[chunk, region, :, columns[chunk]],
            send_sem.at[0],
            one_recv_sem.at[chunk, 1],
            peer(1),
        )
    share(2)
    route.finish(far_step)
    route.start(near_step)
    for chunk in range(CHUNKS):
        await_bytes(
            recv_one.at[chunk, pl.ds(far_base, held), :, columns[chunk]],
            one_recv_sem.at[chunk, 1],
        )
        for place in range(held):
            hidden[chunk, place, :, columns[chunk]] = (
                partial[place, :, spans[chunk]]
                + recv_one[chunk, far_base + place, :, columns[chunk]].astype(jnp.float32)
            ).astype(jnp.bfloat16)
        gathers[chunk].start(near_step)

    for step in range(near_step, last_step):
        route.finish(step)
        route.start(step + 1)
        if step + 1 < last_step:
            for chunk in range(CHUNKS):
                gathers[chunk].finish(step)
                gathers[chunk].start(step + 1)

    hidden_width = w_gate.shape[2]
    tiles, tile_rows = activated.shape[1:3]
    tile_blocks = tile_rows // rows
    cuts = [
        slice(start, min(start + TILE, hidden_width)) for start in range(0, hidden_width, TILE)
    ]

    def over_tiles(step):
        if tiles == 1:
            step(0)
        else:
            pl.loop(0, tiles)(step)

    def weigh(tile):
        table = routing[pl.ds(tile * tile_blocks, tile_blocks)].reshape(
            tile_rows, routing.shape[2]
        )
        experts = lax.broadcasted_iota(jnp.int32, table.shape, 1)
        for number, expert in enumerate((me, twin)):
            weight = jnp.sum(jnp.where(experts == expert, table, 0.0), axis=1, keepdims=True)
            row_weight[number, tile] = jnp.broadcast_to(weight, (tile_rows, LANES))

    for chunk in range(CHUNKS):
        gathers[chunk].finish(last_step)
        if chunk == 0:
            for number, weights in enumerate((w_gate, w_up)):
                loads[8 + number].wait()
                await_bytes(weights.at[1], twin_recv_sem.at[number])

        def accumulate(tile, chunk=chunk):
            span = spans[chunk]
            taken = hidden[chunk, pl.ds(tile * tile_blocks, tile_blocks), :, columns[chunk]]
            taken = taken.reshape(tile_rows, span.stop - span.start)
            for number in range(2):
                for cut in cuts:
                    for sums, weights in ((gate_sum, w_gate), (up_sum, w_up)):
                        part = jnp.dot(
                            taken,
                            weights[number, span, cut],
                            preferred_element_type=jnp.float32,
                        )
                        if chunk == 0:
                            sums[number, tile, :, cut] = part
                        else:
                            sums[number, tile, :, cut] += part

        over_tiles(accumulate)
        if chunk == 0:
            route.finish(last_step)
            over_tiles(weigh)

    def activate(tile):
        for number in range(2):
            for cut in cuts:
                gate = gate_sum[number, tile, :, cut]
                activated[number, tile, :, cut] = (
                    gate / (1.0 + jnp.exp(-gate)) * up_sum[number, tile, :, cut]
                ).astype(jnp.bfloat16)

    over_tiles(activate)
    loads[10].wait()
    await_bytes(w_down.at[1], twin_recv_sem.at[2])

    def down(chunk, tile):
        total = None
        for number in range(2):
            made = jnp.dot(
                activated[number, tile],
                w_down[number, :, back_spans[chunk]],
                preferred_element_type=jnp.float32,
            )
            weighed = made * jnp.concatenate(
                [row_weight[number, tile]] * (made.shape[1] // LANES), axis=1
            )
            total = weighed if total is None else total + weighed
        return total.reshape(tile_blocks, rows, total.shape[1])

    for chunk in range(len(BACK)):
        made = [down(chunk, tile) for tile in range(tiles)]
        second_sum.start(
            chunk, 0, lambda place: made[place // tile_blocks][place % tile_blocks]
        )
    for turn in range(len(rounds)):
        for chunk in range(len(BACK)):
            turns = len(plans[chunk])
            if turn >= turns:
                continue
            second_sum.finish(chunk, turn)
            if turn + 1 < turns:
                second_sum.start(
                    chunk, turn + 1, functools.partial(second_sum.value, chunk, turn)
                )
            else:
                out[:, back_spans[chunk]] = second_sum.value(chunk, turn, 0).astype(jnp.bfloat16)
    for chunk in range(CHUNKS):
        await_bytes(send_one.at[chunk, :, :, columns[chunk]], send_sem.at[0])
    for chunk, span in enumerate(back_spans):
        await_bytes(send_two.at[chunk, :, :, pl.ds(0, span.stop - span.start)], send_sem.at[1])
    given = sum(
        ((1 << len(groups[step])) - 1) << starts[step] for step in range(near_step, last_step + 1)
    )
    for chunk in range(CHUNKS):
        await_bytes(hidden.at[chunk, pl.ds(0, given), :, columns[chunk]], send_sem.at[2])
    await_bytes(routing.at[pl.ds(1, places - 1)], send_sem.at[3])
    for number, weights in enumerate((w_gate, w_up, w_down)):
        await_bytes(weights.at[0], twin_send_sem.at[number])


def body(
    queries,
    tree_kv,
    kv_cache,
    block_table,
    cache_lengths,
    parents,
    w_out,
    w_gate,
    w_up,
    w_down,
    expert_ids,
    gate_weights,
):
    count = lax.axis_size("wide")
    rows = expert_ids.shape[0]
    features = w_out.shape[1]
    hidden_width = w_gate.shape[2]
    slices = queries.shape[0] // rows
    groups, starts, slice_shift = layout(count, slices)
    front, back = widest_of(features, FRONT), widest_of(features, BACK)
    lanes = -(-count // LANES) * LANES
    places = 1 << starts[-1]
    tile_rows = min(TILE, places * rows)
    tiles = places * rows // tile_rows
    hbm = pl.BlockSpec(memory_space=pl.ANY)
    vmem = pl.BlockSpec(memory_space=pltpu.VMEM)
    dma = pltpu.SemaphoreType.DMA
    ids, weights_of = expert_ids.T, gate_weights.T
    return pl.pallas_call(
        functools.partial(layer_kernel, count),
        out_shape=pltpu.VMEM((rows, features), jnp.bfloat16),
        in_specs=[hbm] * 12,
        out_specs=vmem,
        scratch_shapes=[
            pltpu.SMEM(block_table.shape, block_table.dtype),
            pltpu.SMEM(cache_lengths.shape, cache_lengths.dtype),
            pltpu.VMEM(parents.shape, parents.dtype),
            pltpu.VMEM(ids.shape, ids.dtype),
            pltpu.VMEM(weights_of.shape, weights_of.dtype),
            pltpu.VMEM(queries.shape, queries.dtype),
            pltpu.VMEM(tree_kv.shape, tree_kv.dtype),
            pltpu.VMEM(kv_cache.shape, kv_cache.dtype),
            pltpu.VMEM(w_out.shape, w_out.dtype),
            pltpu.VMEM((2, *w_gate.shape[1:]), w_gate.dtype),
            pltpu.VMEM((2, *w_up.shape[1:]), w_up.dtype),
            pltpu.VMEM((2, *w_down.shape[1:]), w_down.dtype),
            pltpu.VMEM((slices, rows, queries.shape[1]), jnp.bfloat16),
            pltpu.VMEM((1 << starts[1], rows, features), jnp.float32),
            pltpu.VMEM((CHUNKS, places, rows, front), jnp.bfloat16),
            pltpu.VMEM((places, rows, lanes), jnp.float32),
            pltpu.VMEM((2, tiles, tile_rows, LANES), jnp.float32),
            pltpu.VMEM((2, tiles, tile_rows, hidden_width), jnp.float32),
            pltpu.VMEM((2, tiles, tile_rows, hidden_width), jnp.float32),
            pltpu.VMEM((2, tiles, tile_rows, hidden_width), jnp.bfloat16),
            pltpu.VMEM((1 << starts[-2], rows, features), jnp.float32),
            pltpu.VMEM((CHUNKS, slices, rows, front), jnp.bfloat16),
            pltpu.VMEM((CHUNKS, slices, rows, front), jnp.bfloat16),
            pltpu.VMEM((len(BACK), places - 1, rows, back), jnp.bfloat16),
            pltpu.VMEM((len(BACK), places - 1, rows, back), jnp.bfloat16),
            dma((11 + CHUNKS,)),
            dma((4,)),
            dma((CHUNKS, 2)),
            dma((CHUNKS, len(groups))),
            dma((len(groups),)),
            dma((len(BACK), len(groups))),
            dma((3,)),
            dma((3,)),
        ],
        compiler_params=pltpu.CompilerParams(
            collective_id=0, has_side_effects=True, vmem_limit_bytes=60 << 20
        ),
    )(
        block_table,
        cache_lengths,
        queries,
        tree_kv,
        kv_cache,
        parents,
        w_out,
        w_gate,
        w_up,
        w_down,
        ids,
        weights_of,
    )


def solution(mesh):
    placed = (
        P(("groups", "wide"), None),
        P(None, ("groups", "wide"), None),
        P(None, ("groups", "wide"), None, None),
        P(("groups", "wide"), None),
        P(("groups", "wide"), None),
        P(("groups", "wide"), None),
        P("wide", None),
        P("wide", None, None),
        P("wide", None, None),
        P("wide", None, None),
        P(("groups", "wide"), None),
        P(("groups", "wide"), None),
    )
    return jax.shard_map(
        body, mesh=mesh, in_specs=placed, out_specs=P(("groups", "wide"), None), check_vma=False
    )
```

```python
import functools

import jax
import jax.numpy as jnp
from jax import lax
from jax.experimental import pallas as pl
from jax.experimental.pallas import tpu as pltpu
from jax.sharding import PartitionSpec as P

FRONT = (3, 5, 5, 3)
BACK = (4, 4, 4, 4)
DIRECT = 2
CHUNKS = len(FRONT)
TILE = 256
LANES = 128
MESH = pl.DeviceIdType.MESH


def layout(count, slices):
    bits = list(range(count.bit_length() - 1))
    shift = len(bits) - (slices.bit_length() - 1)
    far, near = bits[-1:], bits[shift:-1]
    groups = [tuple(far), tuple(near)]
    low = bits[1:shift]
    while low:
        groups.append(tuple(low[-2:]))
        low = low[:-2]
    groups = [group for group in groups if group]
    starts = [0]
    for group in groups:
        starts.append(starts[-1] + len(group))
    return groups, starts, shift


def second_plans(starts):
    plan = list(zip(starts, starts[1:]))[::-1]
    short = [(0, starts[-1])] if len(starts) == 3 else plan
    return [short if chunk >= len(BACK) - DIRECT else plan for chunk in range(len(BACK))]


def shares_of(features, shares):
    spans, start = [], 0
    for share in shares:
        stop = start + share * features // sum(shares)
        spans.append(slice(start, stop))
        start = stop
    return spans


def widest_of(features, shares):
    return max(span.stop - span.start for span in shares_of(features, shares))


def farthest_first(low, high):
    def distance(place):
        return (-(place & 1), -bin(place).count("1"), place)

    return sorted(range(1 << low, 1 << high, 1 << low), key=distance)


def layer_kernel(
    count,
    block_table_in,
    cache_lengths_in,
    queries_in,
    tree_in,
    cache_in,
    parents_in,
    w_out_in,
    w_gate_in,
    w_up_in,
    w_down_in,
    expert_ids_in,
    gate_weights_in,
    out,
    block_table,
    cache_lengths,
    parents,
    expert_ids,
    gate_weights,
    queries,
    tree,
    cache,
    w_out,
    w_gate,
    w_up,
    w_down,
    attended,
    partial,
    hidden,
    routing,
    row_weight,
    gate_sum,
    up_sum,
    activated,
    produced,
    send_one,
    recv_one,
    send_two,
    recv_two,
    load_sem,
    send_sem,
    one_recv_sem,
    all_recv_sem,
    route_recv_sem,
    two_recv_sem,
    twin_send_sem,
    twin_recv_sem,
):
    me = lax.axis_index("wide")
    rows = out.shape[0]
    slices = attended.shape[0]
    groups, starts, slice_shift = layout(count, slices)
    places = 1 << starts[-1]
    mine = [(me // (1 << bit)) % 2 for bit in range(starts[-1] + 1)]
    twin = me + 1 - 2 * mine[0]

    order = [bit for group in groups for bit in group]

    def peer(place):
        device = me
        for number, bit in enumerate(order):
            if place >> number & 1:
                device = device + (1 - 2 * mine[bit]) * (1 << bit)
        return device

    rounds = list(zip(starts, starts[1:]))
    plans = second_plans(starts)
    friends = sorted(
        {
            pattern << low
            for low, high in sum(plans, rounds)
            for pattern in range(1, 1 << (high - low))
        }
    )
    friends = [twin] + [peer(place) for place in friends]
    barrier = pltpu.get_barrier_semaphore()
    for friend in friends:
        pl.semaphore_signal(barrier, inc=1, device_id={"wide": friend}, device_id_type=MESH)

    loads = []
    for number, (source, target) in enumerate(
        (
            (parents_in, parents),
            (queries_in, queries),
            (tree_in, tree),
            (cache_in, cache),
            (block_table_in, block_table),
            (cache_lengths_in, cache_lengths),
            (expert_ids_in, expert_ids),
            (gate_weights_in, gate_weights),
            (w_gate_in.at[0], w_gate.at[0]),
            (w_up_in.at[0], w_up.at[0]),
            (w_down_in.at[0], w_down.at[0]),
        )
    ):
        copy = pltpu.make_async_copy(source, target, load_sem.at[number])
        if number < 6:
            copy.start()
        loads.append(copy)
    out_loads = []
    for number, span in enumerate(shares_of(w_out.shape[1], FRONT)):
        view = (slice(None), pl.ds(span.start, span.stop - span.start))
        out_loads.append(
            pltpu.make_async_copy(w_out_in.at[view], w_out.at[view], load_sem.at[11 + number])
        )

    seq_count, node_count = parents.shape
    head_dim = tree.shape[2]
    head_count = queries.shape[1] // head_dim
    page_count = block_table.shape[1]
    node_rows = lax.broadcasted_iota(jnp.int32, (node_count, node_count), 0)
    node_cols = lax.broadcasted_iota(jnp.int32, (node_count, node_count), 1)
    loads[0].wait()
    for copy in out_loads + loads[6:8]:
        copy.start()
    closures = []
    for seq in range(seq_count):
        linked = ((parents[seq : seq + 1, :] == node_rows) | (node_rows == node_cols)).astype(
            jnp.float32
        )
        closures.append(linked)
    for repeat in range(max(node_count - 1, 1).bit_length()):
        narrow = [linked.astype(jnp.bfloat16) for linked in closures]
        closures = [
            jnp.dot(linked, linked, preferred_element_type=jnp.float32) for linked in narrow
        ]

    def relative_slice(place):
        index = 0
        for group, start in zip(groups, starts):
            for number, bit in enumerate(group):
                if bit >= slice_shift:
                    fixed = place >> (bit - slice_shift) & 1
                    index = index + (1 - mine[bit] if fixed else mine[bit]) * (
                        1 << (start + number)
                    )
        return index

    def send(source, target, send_sem, recv_sem, device):
        pltpu.make_async_remote_copy(
            src_ref=source,
            dst_ref=target,
            send_sem=send_sem,
            recv_sem=recv_sem,
            device_id={"wide": device},
            device_id_type=MESH,
        ).start()

    def await_bytes(view, sem):
        pltpu.make_async_copy(view, view, sem).wait()

    shared = ((w_gate_in, w_gate), (w_up_in, w_up), (w_down_in, w_down))

    def share(number):
        source, target = shared[number]
        send(source.at[0], target.at[1], twin_send_sem.at[number], twin_recv_sem.at[number], twin)

    for copy in loads[1:6]:
        copy.wait()
    cached = page_count * cache.shape[2]
    positions = lax.broadcasted_iota(jnp.int32, (head_count * node_count, cached), 1)
    across = (((1,), (1,)), ((), ()))
    for seq in range(seq_count):
        first = seq * node_count
        last = first + node_count
        stacked = jnp.concatenate(
            [
                queries[first:last, head * head_dim : (head + 1) * head_dim]
                for head in range(head_count)
            ],
            axis=0,
        )
        pages = [block_table[seq, page] for page in range(page_count)]
        keys = jnp.concatenate([cache[0, page] for page in pages], axis=0)
        values = jnp.concatenate([cache[1, page] for page in pages], axis=0)
        scale = head_dim ** (-0.5)
        cache_scores = (
            lax.dot_general(stacked, keys, across, preferred_element_type=jnp.float32) * scale
        )
        tree_scores = (
            lax.dot_general(
                stacked, tree[0, first:last], across, preferred_element_type=jnp.float32
            )
            * scale
        )
        seen = jnp.concatenate([closures[seq].T] * head_count, axis=0) > 0.5
        cache_scores = jnp.where(positions < cache_lengths[0, seq], cache_scores, -jnp.inf)
        tree_scores = jnp.where(seen, tree_scores, -jnp.inf)
        highest = jnp.maximum(
            jnp.max(cache_scores, axis=1, keepdims=True),
            jnp.max(tree_scores, axis=1, keepdims=True),
        )
        cache_probs = jnp.exp(cache_scores - highest)
        tree_probs = jnp.exp(tree_scores - highest)
        denominator = jnp.sum(cache_probs, axis=1, keepdims=True) + jnp.sum(
            tree_probs, axis=1, keepdims=True
        )
        blended = jnp.dot(
            cache_probs.astype(jnp.bfloat16), values, preferred_element_type=jnp.float32
        ) + jnp.dot(
            tree_probs.astype(jnp.bfloat16),
            tree[1, first:last],
            preferred_element_type=jnp.float32,
        )
        blended = (blended / denominator).astype(jnp.bfloat16)
        for part in range(node_count // rows):
            index = relative_slice((first + part * rows) // rows)
            for head in range(head_count):
                top = head * node_count + part * rows
                attended[index, :, head * head_dim : (head + 1) * head_dim] = blended[
                    top : top + rows
                ]

    spans = shares_of(w_out.shape[1], FRONT)
    columns = [pl.ds(0, span.stop - span.start) for span in spans]
    back_spans = shares_of(w_out.shape[1], BACK)

    class Gather:
        def __init__(self, buffer, send_sem, recv_sems, skipped):
            self.skipped = skipped
            self.buffer = buffer
            self.send_sem = send_sem
            self.recv_sems = recv_sems

        def start(self, step):
            held = 1 << starts[step]
            for place in farthest_first(*rounds[step]):
                send(
                    self.buffer.at[pl.ds(0, held)],
                    self.buffer.at[pl.ds(place, held)],
                    self.send_sem,
                    self.recv_sems.at[step - self.skipped],
                    peer(place),
                )

        def finish(self, step):
            held = 1 << starts[step]
            region = pl.ds(held, (1 << starts[step + 1]) - held)
            await_bytes(self.buffer.at[region], self.recv_sems.at[step - self.skipped])

    class Scatter:
        def __init__(self, kept, out_buffer, in_buffer, send_sem, recv_sems, plans, spans):
            self.spans = spans
            self.kept = kept
            self.out_buffer = out_buffer
            self.in_buffer = in_buffer
            self.send_sem = send_sem
            self.recv_sems = recv_sems
            self.plans = plans
            self.columns = [pl.ds(0, span.stop - span.start) for span in spans]

        def slot(self, chunk, turn, place):
            plan = self.plans[chunk]
            first = sum((1 << high) - (1 << low) for low, high in plan[:turn])
            return first + place - (1 << plan[turn][0])

        def launch(self, chunk, turn, place):
            held = 1 << self.plans[chunk][turn][0]
            region = pl.ds(self.slot(chunk, turn, place), held)
            send(
                self.out_buffer.at[chunk, region, :, self.columns[chunk]],
                self.in_buffer.at[chunk, region, :, self.columns[chunk]],
                self.send_sem,
                self.recv_sems.at[chunk, turn],
                peer(place),
            )

        def start(self, chunk, turn, value):
            low, high = self.plans[chunk][turn]
            for first in farthest_first(low, high):
                for place in range(first, first + (1 << low)):
                    self.out_buffer[
                        chunk, self.slot(chunk, turn, place), :, self.columns[chunk]
                    ] = value(place).astype(jnp.bfloat16)
                self.launch(chunk, turn, first)
            for place in range(1 << low):
                self.kept[place, :, self.spans[chunk]] = value(place)

        def finish(self, chunk, turn):
            low, high = self.plans[chunk][turn]
            region = pl.ds(self.slot(chunk, turn, 1 << low), (1 << high) - (1 << low))
            await_bytes(
                self.in_buffer.at[chunk, region, :, self.columns[chunk]],
                self.recv_sems.at[chunk, turn],
            )

        def value(self, chunk, turn, place):
            low, high = self.plans[chunk][turn]
            total = self.kept[place, :, self.spans[chunk]]
            for first in range(1 << low, 1 << high, 1 << low):
                total = total + self.in_buffer[
                    chunk, self.slot(chunk, turn, first + place), :, self.columns[chunk]
                ].astype(jnp.float32)
            return total

    far_step, near_step, last_step = 0, 1, len(groups) - 1
    first_sum = Scatter(partial, send_one, recv_one, send_sem.at[0], one_recv_sem,
        [[rounds[near_step]]] * CHUNKS, spans,
    )
    second_sum = Scatter(
        produced, send_two, recv_two, send_sem.at[1], two_recv_sem,
        plans, back_spans,
    )
    gathers = [
        Gather(hidden.at[chunk, :, :, columns[chunk]], send_sem.at[2], all_recv_sem.at[chunk], 1)
        for chunk in range(CHUNKS)
    ]
    route = Gather(routing, send_sem.at[3], route_recv_sem, 0)

    for chunk in range(CHUNKS):
        out_loads[chunk].wait()
        projected = jnp.dot(
            attended[...].reshape(slices * rows, attended.shape[2]),
            w_out[:, spans[chunk]],
            preferred_element_type=jnp.float32,
        )
        if chunk == 0:
            pl.semaphore_wait(barrier, len(friends))
            share(0)
            share(1)
        first_sum.start(
            chunk, 0, lambda place: projected[place * rows : (place + 1) * rows]
        )
    loads[6].wait()
    loads[7].wait()
    ids = expert_ids[...].T
    weights_of = gate_weights[...].T
    lane_ids = lax.broadcasted_iota(jnp.int32, (rows, routing.shape[2]), 1)
    listed = jnp.zeros((rows, routing.shape[2]), jnp.float32)
    for k in range(expert_ids.shape[0]):
        listed += jnp.where(ids[:, k : k + 1] == lane_ids, weights_of[:, k : k + 1], 0.0)
    routing[0] = listed

    route.start(far_step)
    for copy in loads[8:]:
        copy.start()

    held = 1 << starts[near_step]
    far_base = (slices - held)
    for chunk in range(CHUNKS):
        first_sum.finish(chunk, 0)
        for place in range(held):
            value = first_sum.value(chunk, 0, place)
            partial[place, :, spans[chunk]] = value
            send_one[chunk, far_base + held - 1 - place, :, columns[chunk]] = value.astype(
                jnp.bfloat16
            )
        region = pl.ds(far_base, held)
        send(
            send_one.at[chunk, region, :, columns[chunk]],
            recv_one.at[chunk, region, :, columns[chunk]],
            send_sem.at[0],
            one_recv_sem.at[chunk, 1],
            peer(1),
        )
    share(2)
    route.finish(far_step)
    route.start(near_step)
    for chunk in range(CHUNKS):
        await_bytes(
            recv_one.at[chunk, pl.ds(far_base, held), :, columns[chunk]],
            one_recv_sem.at[chunk, 1],
        )
        for place in range(held):
            hidden[chunk, place, :, columns[chunk]] = (
                partial[place, :, spans[chunk]]
                + recv_one[chunk, far_base + place, :, columns[chunk]].astype(jnp.float32)
            ).astype(jnp.bfloat16)
        gathers[chunk].start(near_step)

    for step in range(near_step, last_step):
        route.finish(step)
        route.start(step + 1)
        if step + 1 < last_step:
            for chunk in range(CHUNKS):
                gathers[chunk].finish(step)
                gathers[chunk].start(step + 1)

    hidden_width = w_gate.shape[2]
    tiles, tile_rows = activated.shape[1:3]
    tile_blocks = tile_rows // rows
    cuts = [
        slice(start, min(start + TILE, hidden_width)) for start in range(0, hidden_width, TILE)
    ]

    def over_tiles(step):
        if tiles == 1:
            step(0)
        else:
            pl.loop(0, tiles)(step)

    def weigh(tile):
        table = routing[pl.ds(tile * tile_blocks, tile_blocks)].reshape(
            tile_rows, routing.shape[2]
        )
        experts = lax.broadcasted_iota(jnp.int32, table.shape, 1)
        for number, expert in enumerate((me, twin)):
            weight = jnp.sum(jnp.where(experts == expert, table, 0.0), axis=1, keepdims=True)
            row_weight[number, tile] = jnp.broadcast_to(weight, (tile_rows, LANES))

    for chunk in range(CHUNKS):
        gathers[chunk].finish(last_step)
        if chunk == 0:
            for number, weights in enumerate((w_gate, w_up)):
                loads[8 + number].wait()
                await_bytes(weights.at[1], twin_recv_sem.at[number])

        def accumulate(tile, chunk=chunk):
            span = spans[chunk]
            taken = hidden[chunk, pl.ds(tile * tile_blocks, tile_blocks), :, columns[chunk]]
            taken = taken.reshape(tile_rows, span.stop - span.start)
            for number in range(2):
                for cut in cuts:
                    for sums, weights in ((gate_sum, w_gate), (up_sum, w_up)):
                        part = jnp.dot(
                            taken,
                            weights[number, span, cut],
                            preferred_element_type=jnp.float32,
                        )
                        if chunk == 0:
                            sums[number, tile, :, cut] = part
                        else:
                            sums[number, tile, :, cut] += part

        over_tiles(accumulate)
        if chunk == 0:
            route.finish(last_step)
            over_tiles(weigh)

    def activate(tile):
        for number in range(2):
            for cut in cuts:
                gate = gate_sum[number, tile, :, cut]
                activated[number, tile, :, cut] = (
                    gate / (1.0 + jnp.exp(-gate)) * up_sum[number, tile, :, cut]
                ).astype(jnp.bfloat16)

    over_tiles(activate)
    loads[10].wait()
    await_bytes(w_down.at[1], twin_recv_sem.at[2])

    def down(chunk, tile):
        total = None
        for number in range(2):
            made = jnp.dot(
                activated[number, tile],
                w_down[number, :, back_spans[chunk]],
                preferred_element_type=jnp.float32,
            )
            weighed = made * jnp.concatenate(
                [row_weight[number, tile]] * (made.shape[1] // LANES), axis=1
            )
            total = weighed if total is None else total + weighed
        return total.reshape(tile_blocks, rows, total.shape[1])

    for chunk in range(len(BACK)):
        made = [down(chunk, tile) for tile in range(tiles)]
        second_sum.start(
            chunk, 0, lambda place: made[place // tile_blocks][place % tile_blocks]
        )
    for turn in range(len(rounds)):
        for chunk in range(len(BACK)):
            turns = len(plans[chunk])
            if turn >= turns:
                continue
            second_sum.finish(chunk, turn)
            if turn + 1 < turns:
                second_sum.start(
                    chunk, turn + 1, functools.partial(second_sum.value, chunk, turn)
                )
            else:
                out[:, back_spans[chunk]] = second_sum.value(chunk, turn, 0).astype(jnp.bfloat16)
    for chunk in range(CHUNKS):
        await_bytes(send_one.at[chunk, :, :, columns[chunk]], send_sem.at[0])
    for chunk, span in enumerate(back_spans):
        await_bytes(send_two.at[chunk, :, :, pl.ds(0, span.stop - span.start)], send_sem.at[1])
    given = sum(
        ((1 << len(groups[step])) - 1) << starts[step] for step in range(near_step, last_step + 1)
    )
    for chunk in range(CHUNKS):
        await_bytes(hidden.at[chunk, pl.ds(0, given), :, columns[chunk]], send_sem.at[2])
    await_bytes(routing.at[pl.ds(1, places - 1)], send_sem.at[3])
    for number, weights in enumerate((w_gate, w_up, w_down)):
        await_bytes(weights.at[0], twin_send_sem.at[number])


def body(
    queries,
    tree_kv,
    kv_cache,
    block_table,
    cache_lengths,
    parents,
    w_out,
    w_gate,
    w_up,
    w_down,
    expert_ids,
    gate_weights,
):
    count = lax.axis_size("wide")
    rows = expert_ids.shape[0]
    features = w_out.shape[1]
    hidden_width = w_gate.shape[2]
    slices = queries.shape[0] // rows
    groups, starts, slice_shift = layout(count, slices)
    front, back = widest_of(features, FRONT), widest_of(features, BACK)
    lanes = -(-count // LANES) * LANES
    places = 1 << starts[-1]
    tile_rows = min(TILE, places * rows)
    tiles = places * rows // tile_rows
    hbm = pl.BlockSpec(memory_space=pl.ANY)
    vmem = pl.BlockSpec(memory_space=pltpu.VMEM)
    dma = pltpu.SemaphoreType.DMA
    ids, weights_of = expert_ids.T, gate_weights.T
    return pl.pallas_call(
        functools.partial(layer_kernel, count),
        out_shape=pltpu.VMEM((rows, features), jnp.bfloat16),
        in_specs=[hbm] * 12,
        out_specs=vmem,
        scratch_shapes=[
            pltpu.SMEM(block_table.shape, block_table.dtype),
            pltpu.SMEM(cache_lengths.shape, cache_lengths.dtype),
            pltpu.VMEM(parents.shape, parents.dtype),
            pltpu.VMEM(ids.shape, ids.dtype),
            pltpu.VMEM(weights_of.shape, weights_of.dtype),
            pltpu.VMEM(queries.shape, queries.dtype),
            pltpu.VMEM(tree_kv.shape, tree_kv.dtype),
            pltpu.VMEM(kv_cache.shape, kv_cache.dtype),
            pltpu.VMEM(w_out.shape, w_out.dtype),
            pltpu.VMEM((2, *w_gate.shape[1:]), w_gate.dtype),
            pltpu.VMEM((2, *w_up.shape[1:]), w_up.dtype),
            pltpu.VMEM((2, *w_down.shape[1:]), w_down.dtype),
            pltpu.VMEM((slices, rows, queries.shape[1]), jnp.bfloat16),
            pltpu.VMEM((1 << starts[1], rows, features), jnp.float32),
            pltpu.VMEM((CHUNKS, places, rows, front), jnp.bfloat16),
            pltpu.VMEM((places, rows, lanes), jnp.float32),
            pltpu.VMEM((2, tiles, tile_rows, LANES), jnp.float32),
            pltpu.VMEM((2, tiles, tile_rows, hidden_width), jnp.float32),
            pltpu.VMEM((2, tiles, tile_rows, hidden_width), jnp.float32),
            pltpu.VMEM((2, tiles, tile_rows, hidden_width), jnp.bfloat16),
            pltpu.VMEM((1 << starts[-2], rows, features), jnp.float32),
            pltpu.VMEM((CHUNKS, slices, rows, front), jnp.bfloat16),
            pltpu.VMEM((CHUNKS, slices, rows, front), jnp.bfloat16),
            pltpu.VMEM((len(BACK), places - 1, rows, back), jnp.bfloat16),
            pltpu.VMEM((len(BACK), places - 1, rows, back), jnp.bfloat16),
            dma((11 + CHUNKS,)),
            dma((4,)),
            dma((CHUNKS, 2)),
            dma((CHUNKS, len(groups) - 1)),
            dma((len(groups),)),
            dma((len(BACK), len(groups))),
            dma((3,)),
            dma((3,)),
        ],
        compiler_params=pltpu.CompilerParams(
            collective_id=0, has_side_effects=True, vmem_limit_bytes=60 << 20
        ),
    )(
        block_table,
        cache_lengths,
        queries,
        tree_kv,
        kv_cache,
        parents,
        w_out,
        w_gate,
        w_up,
        w_down,
        ids,
        weights_of,
    )


def solution(mesh):
    placed = (
        P(("groups", "wide"), None),
        P(None, ("groups", "wide"), None),
        P(None, ("groups", "wide"), None, None),
        P(("groups", "wide"), None),
        P(("groups", "wide"), None),
        P(("groups", "wide"), None),
        P("wide", None),
        P("wide", None, None),
        P("wide", None, None),
        P("wide", None, None),
        P(("groups", "wide"), None),
        P(("groups", "wide"), None),
    )
    return jax.shard_map(
        body, mesh=mesh, in_specs=placed, out_specs=P(("groups", "wide"), None), check_vma=False
    )
```

```python
import functools

import jax
import jax.numpy as jnp
from jax import lax
from jax.experimental import pallas as pl
from jax.experimental.pallas import tpu as pltpu
from jax.sharding import PartitionSpec as P

FRONT = (2, 4, 4, 4, 2)
BACK = (4, 4, 4, 4)
DIRECT = 2
CHUNKS = len(FRONT)
TILE = 256
LANES = 128
MESH = pl.DeviceIdType.MESH


def layout(count, slices):
    bits = list(range(count.bit_length() - 1))
    shift = len(bits) - (slices.bit_length() - 1)
    far, near = bits[-1:], bits[shift:-1]
    groups = [tuple(far), tuple(near)]
    low = bits[1:shift]
    while low:
        groups.append(tuple(low[-2:]))
        low = low[:-2]
    groups = [group for group in groups if group]
    starts = [0]
    for group in groups:
        starts.append(starts[-1] + len(group))
    return groups, starts, shift


def second_plans(starts):
    plan = list(zip(starts, starts[1:]))[::-1]
    short = [(0, starts[-1])] if len(starts) == 3 else plan
    return [short if chunk >= len(BACK) - DIRECT else plan for chunk in range(len(BACK))]


def shares_of(features, shares):
    spans, start = [], 0
    for share in shares:
        stop = start + share * features // sum(shares)
        spans.append(slice(start, stop))
        start = stop
    return spans


def widest_of(features, shares):
    return max(span.stop - span.start for span in shares_of(features, shares))


def farthest_first(low, high):
    def distance(place):
        return (-(place & 1), -bin(place).count("1"), place)

    return sorted(range(1 << low, 1 << high, 1 << low), key=distance)


def layer_kernel(
    count,
    block_table_in,
    cache_lengths_in,
    queries_in,
    tree_in,
    cache_in,
    parents_in,
    w_out_in,
    w_gate_in,
    w_up_in,
    w_down_in,
    expert_ids_in,
    gate_weights_in,
    out,
    block_table,
    cache_lengths,
    parents,
    expert_ids,
    gate_weights,
    queries,
    tree,
    cache,
    w_out,
    w_gate,
    w_up,
    w_down,
    attended,
    partial,
    hidden,
    routing,
    row_weight,
    gate_sum,
    up_sum,
    activated,
    produced,
    send_one,
    recv_one,
    send_two,
    recv_two,
    load_sem,
    send_sem,
    one_recv_sem,
    all_recv_sem,
    route_recv_sem,
    two_recv_sem,
    twin_send_sem,
    twin_recv_sem,
):
    me = lax.axis_index("wide")
    rows = out.shape[0]
    slices = attended.shape[0]
    groups, starts, slice_shift = layout(count, slices)
    places = 1 << starts[-1]
    mine = [(me // (1 << bit)) % 2 for bit in range(starts[-1] + 1)]
    twin = me + 1 - 2 * mine[0]

    order = [bit for group in groups for bit in group]

    def peer(place):
        device = me
        for number, bit in enumerate(order):
            if place >> number & 1:
                device = device + (1 - 2 * mine[bit]) * (1 << bit)
        return device

    rounds = list(zip(starts, starts[1:]))
    plans = second_plans(starts)
    friends = sorted(
        {
            pattern << low
            for low, high in sum(plans, rounds)
            for pattern in range(1, 1 << (high - low))
        }
    )
    friends = [twin] + [peer(place) for place in friends]
    barrier = pltpu.get_barrier_semaphore()
    for friend in friends:
        pl.semaphore_signal(barrier, inc=1, device_id={"wide": friend}, device_id_type=MESH)

    loads = []
    for number, (source, target) in enumerate(
        (
            (parents_in, parents),
            (queries_in, queries),
            (tree_in, tree),
            (cache_in, cache),
            (block_table_in, block_table),
            (cache_lengths_in, cache_lengths),
            (expert_ids_in, expert_ids),
            (gate_weights_in, gate_weights),
            (w_gate_in.at[0], w_gate.at[0]),
            (w_up_in.at[0], w_up.at[0]),
            (w_down_in.at[0], w_down.at[0]),
        )
    ):
        copy = pltpu.make_async_copy(source, target, load_sem.at[number])
        if number < 6:
            copy.start()
        loads.append(copy)
    out_loads = []
    for number, span in enumerate(shares_of(w_out.shape[1], FRONT)):
        view = (slice(None), pl.ds(span.start, span.stop - span.start))
        out_loads.append(
            pltpu.make_async_copy(w_out_in.at[view], w_out.at[view], load_sem.at[11 + number])
        )

    seq_count, node_count = parents.shape
    head_dim = tree.shape[2]
    head_count = queries.shape[1] // head_dim
    page_count = block_table.shape[1]
    node_rows = lax.broadcasted_iota(jnp.int32, (node_count, node_count), 0)
    node_cols = lax.broadcasted_iota(jnp.int32, (node_count, node_count), 1)
    loads[0].wait()
    for copy in out_loads + loads[6:8]:
        copy.start()
    closures = []
    for seq in range(seq_count):
        linked = ((parents[seq : seq + 1, :] == node_rows) | (node_rows == node_cols)).astype(
            jnp.float32
        )
        closures.append(linked)
    for repeat in range(max(node_count - 1, 1).bit_length()):
        narrow = [linked.astype(jnp.bfloat16) for linked in closures]
        closures = [
            jnp.dot(linked, linked, preferred_element_type=jnp.float32) for linked in narrow
        ]

    def relative_slice(place):
        index = 0
        for group, start in zip(groups, starts):
            for number, bit in enumerate(group):
                if bit >= slice_shift:
                    fixed = place >> (bit - slice_shift) & 1
                    index = index + (1 - mine[bit] if fixed else mine[bit]) * (
                        1 << (start + number)
                    )
        return index

    def send(source, target, send_sem, recv_sem, device):
        pltpu.make_async_remote_copy(
            src_ref=source,
            dst_ref=target,
            send_sem=send_sem,
            recv_sem=recv_sem,
            device_id={"wide": device},
            device_id_type=MESH,
        ).start()

    def await_bytes(view, sem):
        pltpu.make_async_copy(view, view, sem).wait()

    shared = ((w_gate_in, w_gate), (w_up_in, w_up), (w_down_in, w_down))

    def share(number):
        source, target = shared[number]
        send(source.at[0], target.at[1], twin_send_sem.at[number], twin_recv_sem.at[number], twin)

    for copy in loads[1:6]:
        copy.wait()
    cached = page_count * cache.shape[2]
    positions = lax.broadcasted_iota(jnp.int32, (head_count * node_count, cached), 1)
    across = (((1,), (1,)), ((), ()))
    for seq in range(seq_count):
        first = seq * node_count
        last = first + node_count
        stacked = jnp.concatenate(
            [
                queries[first:last, head * head_dim : (head + 1) * head_dim]
                for head in range(head_count)
            ],
            axis=0,
        )
        pages = [block_table[seq, page] for page in range(page_count)]
        keys = jnp.concatenate([cache[0, page] for page in pages], axis=0)
        values = jnp.concatenate([cache[1, page] for page in pages], axis=0)
        scale = head_dim ** (-0.5)
        cache_scores = (
            lax.dot_general(stacked, keys, across, preferred_element_type=jnp.float32) * scale
        )
        tree_scores = (
            lax.dot_general(
                stacked, tree[0, first:last], across, preferred_element_type=jnp.float32
            )
            * scale
        )
        seen = jnp.concatenate([closures[seq].T] * head_count, axis=0) > 0.5
        cache_scores = jnp.where(positions < cache_lengths[0, seq], cache_scores, -jnp.inf)
        tree_scores = jnp.where(seen, tree_scores, -jnp.inf)
        highest = jnp.maximum(
            jnp.max(cache_scores, axis=1, keepdims=True),
            jnp.max(tree_scores, axis=1, keepdims=True),
        )
        cache_probs = jnp.exp(cache_scores - highest)
        tree_probs = jnp.exp(tree_scores - highest)
        denominator = jnp.sum(cache_probs, axis=1, keepdims=True) + jnp.sum(
            tree_probs, axis=1, keepdims=True
        )
        blended = jnp.dot(
            cache_probs.astype(jnp.bfloat16), values, preferred_element_type=jnp.float32
        ) + jnp.dot(
            tree_probs.astype(jnp.bfloat16),
            tree[1, first:last],
            preferred_element_type=jnp.float32,
        )
        blended = (blended / denominator).astype(jnp.bfloat16)
        for part in range(node_count // rows):
            index = relative_slice((first + part * rows) // rows)
            for head in range(head_count):
                top = head * node_count + part * rows
                attended[index, :, head * head_dim : (head + 1) * head_dim] = blended[
                    top : top + rows
                ]

    spans = shares_of(w_out.shape[1], FRONT)
    columns = [pl.ds(0, span.stop - span.start) for span in spans]
    back_spans = shares_of(w_out.shape[1], BACK)

    class Gather:
        def __init__(self, buffer, send_sem, recv_sems, skipped):
            self.skipped = skipped
            self.buffer = buffer
            self.send_sem = send_sem
            self.recv_sems = recv_sems

        def start(self, step):
            held = 1 << starts[step]
            for place in farthest_first(*rounds[step]):
                send(
                    self.buffer.at[pl.ds(0, held)],
                    self.buffer.at[pl.ds(place, held)],
                    self.send_sem,
                    self.recv_sems.at[step - self.skipped],
                    peer(place),
                )

        def finish(self, step):
            held = 1 << starts[step]
            region = pl.ds(held, (1 << starts[step + 1]) - held)
            await_bytes(self.buffer.at[region], self.recv_sems.at[step - self.skipped])

    class Scatter:
        def __init__(self, kept, out_buffer, in_buffer, send_sem, recv_sems, plans, spans):
            self.spans = spans
            self.kept = kept
            self.out_buffer = out_buffer
            self.in_buffer = in_buffer
            self.send_sem = send_sem
            self.recv_sems = recv_sems
            self.plans = plans
            self.columns = [pl.ds(0, span.stop - span.start) for span in spans]

        def slot(self, chunk, turn, place):
            plan = self.plans[chunk]
            first = sum((1 << high) - (1 << low) for low, high in plan[:turn])
            return first + place - (1 << plan[turn][0])

        def launch(self, chunk, turn, place):
            held = 1 << self.plans[chunk][turn][0]
            region = pl.ds(self.slot(chunk, turn, place), held)
            send(
                self.out_buffer.at[chunk, region, :, self.columns[chunk]],
                self.in_buffer.at[chunk, region, :, self.columns[chunk]],
                self.send_sem,
                self.recv_sems.at[chunk, turn],
                peer(place),
            )

        def start(self, chunk, turn, value):
            low, high = self.plans[chunk][turn]
            for first in farthest_first(low, high):
                for place in range(first, first + (1 << low)):
                    self.out_buffer[
                        chunk, self.slot(chunk, turn, place), :, self.columns[chunk]
                    ] = value(place).astype(jnp.bfloat16)
                self.launch(chunk, turn, first)
            for place in range(1 << low):
                self.kept[place, :, self.spans[chunk]] = value(place)

        def finish(self, chunk, turn):
            low, high = self.plans[chunk][turn]
            region = pl.ds(self.slot(chunk, turn, 1 << low), (1 << high) - (1 << low))
            await_bytes(
                self.in_buffer.at[chunk, region, :, self.columns[chunk]],
                self.recv_sems.at[chunk, turn],
            )

        def value(self, chunk, turn, place):
            low, high = self.plans[chunk][turn]
            total = self.kept[place, :, self.spans[chunk]]
            for first in range(1 << low, 1 << high, 1 << low):
                total = total + self.in_buffer[
                    chunk, self.slot(chunk, turn, first + place), :, self.columns[chunk]
                ].astype(jnp.float32)
            return total

    far_step, near_step, last_step = 0, 1, len(groups) - 1
    first_sum = Scatter(partial, send_one, recv_one, send_sem.at[0], one_recv_sem,
        [[rounds[near_step]]] * CHUNKS, spans,
    )
    second_sum = Scatter(
        produced, send_two, recv_two, send_sem.at[1], two_recv_sem,
        plans, back_spans,
    )
    gathers = [
        Gather(hidden.at[chunk, :, :, columns[chunk]], send_sem.at[2], all_recv_sem.at[chunk], 1)
        for chunk in range(CHUNKS)
    ]
    route = Gather(routing, send_sem.at[3], route_recv_sem, 0)

    for chunk in range(CHUNKS):
        out_loads[chunk].wait()
        projected = jnp.dot(
            attended[...].reshape(slices * rows, attended.shape[2]),
            w_out[:, spans[chunk]],
            preferred_element_type=jnp.float32,
        )
        if chunk == 0:
            pl.semaphore_wait(barrier, len(friends))
            share(0)
            share(1)
        first_sum.start(
            chunk, 0, lambda place: projected[place * rows : (place + 1) * rows]
        )
    loads[6].wait()
    loads[7].wait()
    ids = expert_ids[...].T
    weights_of = gate_weights[...].T
    lane_ids = lax.broadcasted_iota(jnp.int32, (rows, routing.shape[2]), 1)
    listed = jnp.zeros((rows, routing.shape[2]), jnp.float32)
    for k in range(expert_ids.shape[0]):
        listed += jnp.where(ids[:, k : k + 1] == lane_ids, weights_of[:, k : k + 1], 0.0)
    routing[0] = listed

    route.start(far_step)
    for copy in loads[8:]:
        copy.start()

    held = 1 << starts[near_step]
    far_base = (slices - held)
    for chunk in range(CHUNKS):
        first_sum.finish(chunk, 0)
        for place in range(held):
            value = first_sum.value(chunk, 0, place)
            partial[place, :, spans[chunk]] = value
            send_one[chunk, far_base + held - 1 - place, :, columns[chunk]] = value.astype(
                jnp.bfloat16
            )
        region = pl.ds(far_base, held)
        send(
            send_one.at[chunk, region, :, columns[chunk]],
            recv_one.at[chunk, region, :, columns[chunk]],
            send_sem.at[0],
            one_recv_sem.at[chunk, 1],
            peer(1),
        )
    share(2)
    route.finish(far_step)
    route.start(near_step)
    for chunk in range(CHUNKS):
        await_bytes(
            recv_one.at[chunk, pl.ds(far_base, held), :, columns[chunk]],
            one_recv_sem.at[chunk, 1],
        )
        for place in range(held):
            hidden[chunk, place, :, columns[chunk]] = (
                partial[place, :, spans[chunk]]
                + recv_one[chunk, far_base + place, :, columns[chunk]].astype(jnp.float32)
            ).astype(jnp.bfloat16)
        gathers[chunk].start(near_step)

    for step in range(near_step, last_step):
        route.finish(step)
        route.start(step + 1)
        if step + 1 < last_step:
            for chunk in range(CHUNKS):
                gathers[chunk].finish(step)
                gathers[chunk].start(step + 1)

    hidden_width = w_gate.shape[2]
    tiles, tile_rows = activated.shape[1:3]
    tile_blocks = tile_rows // rows
    cuts = [
        slice(start, min(start + TILE, hidden_width)) for start in range(0, hidden_width, TILE)
    ]

    def over_tiles(step):
        if tiles == 1:
            step(0)
        else:
            pl.loop(0, tiles)(step)

    def weigh(tile):
        table = routing[pl.ds(tile * tile_blocks, tile_blocks)].reshape(
            tile_rows, routing.shape[2]
        )
        experts = lax.broadcasted_iota(jnp.int32, table.shape, 1)
        for number, expert in enumerate((me, twin)):
            weight = jnp.sum(jnp.where(experts == expert, table, 0.0), axis=1, keepdims=True)
            row_weight[number, tile] = jnp.broadcast_to(weight, (tile_rows, LANES))

    for chunk in range(CHUNKS):
        gathers[chunk].finish(last_step)
        if chunk == 0:
            for number, weights in enumerate((w_gate, w_up)):
                loads[8 + number].wait()
                await_bytes(weights.at[1], twin_recv_sem.at[number])

        def accumulate(tile, chunk=chunk):
            span = spans[chunk]
            taken = hidden[chunk, pl.ds(tile * tile_blocks, tile_blocks), :, columns[chunk]]
            taken = taken.reshape(tile_rows, span.stop - span.start)
            for number in range(2):
                for cut in cuts:
                    for sums, weights in ((gate_sum, w_gate), (up_sum, w_up)):
                        part = jnp.dot(
                            taken,
                            weights[number, span, cut],
                            preferred_element_type=jnp.float32,
                        )
                        if chunk == 0:
                            sums[number, tile, :, cut] = part
                        else:
                            sums[number, tile, :, cut] += part

        over_tiles(accumulate)
        if chunk == 0:
            route.finish(last_step)
            over_tiles(weigh)

    def activate(tile):
        for number in range(2):
            for cut in cuts:
                gate = gate_sum[number, tile, :, cut]
                activated[number, tile, :, cut] = (
                    gate / (1.0 + jnp.exp(-gate)) * up_sum[number, tile, :, cut]
                ).astype(jnp.bfloat16)

    over_tiles(activate)
    loads[10].wait()
    await_bytes(w_down.at[1], twin_recv_sem.at[2])

    def down(chunk, tile):
        total = None
        for number in range(2):
            made = jnp.dot(
                activated[number, tile],
                w_down[number, :, back_spans[chunk]],
                preferred_element_type=jnp.float32,
            )
            weighed = made * jnp.concatenate(
                [row_weight[number, tile]] * (made.shape[1] // LANES), axis=1
            )
            total = weighed if total is None else total + weighed
        return total.reshape(tile_blocks, rows, total.shape[1])

    for chunk in range(len(BACK)):
        made = [down(chunk, tile) for tile in range(tiles)]
        second_sum.start(
            chunk, 0, lambda place: made[place // tile_blocks][place % tile_blocks]
        )
    for turn in range(len(rounds)):
        for chunk in range(len(BACK)):
            turns = len(plans[chunk])
            if turn >= turns:
                continue
            second_sum.finish(chunk, turn)
            if turn + 1 < turns:
                second_sum.start(
                    chunk, turn + 1, functools.partial(second_sum.value, chunk, turn)
                )
            else:
                out[:, back_spans[chunk]] = second_sum.value(chunk, turn, 0).astype(jnp.bfloat16)
    for chunk in range(CHUNKS):
        await_bytes(send_one.at[chunk, :, :, columns[chunk]], send_sem.at[0])
    for chunk, span in enumerate(back_spans):
        await_bytes(send_two.at[chunk, :, :, pl.ds(0, span.stop - span.start)], send_sem.at[1])
    given = sum(
        ((1 << len(groups[step])) - 1) << starts[step] for step in range(near_step, last_step + 1)
    )
    for chunk in range(CHUNKS):
        await_bytes(hidden.at[chunk, pl.ds(0, given), :, columns[chunk]], send_sem.at[2])
    await_bytes(routing.at[pl.ds(1, places - 1)], send_sem.at[3])
    for number, weights in enumerate((w_gate, w_up, w_down)):
        await_bytes(weights.at[0], twin_send_sem.at[number])


def body(
    queries,
    tree_kv,
    kv_cache,
    block_table,
    cache_lengths,
    parents,
    w_out,
    w_gate,
    w_up,
    w_down,
    expert_ids,
    gate_weights,
):
    count = lax.axis_size("wide")
    rows = expert_ids.shape[0]
    features = w_out.shape[1]
    hidden_width = w_gate.shape[2]
    slices = queries.shape[0] // rows
    groups, starts, slice_shift = layout(count, slices)
    front, back = widest_of(features, FRONT), widest_of(features, BACK)
    lanes = -(-count // LANES) * LANES
    places = 1 << starts[-1]
    tile_rows = min(TILE, places * rows)
    tiles = places * rows // tile_rows
    hbm = pl.BlockSpec(memory_space=pl.ANY)
    vmem = pl.BlockSpec(memory_space=pltpu.VMEM)
    dma = pltpu.SemaphoreType.DMA
    ids, weights_of = expert_ids.T, gate_weights.T
    return pl.pallas_call(
        functools.partial(layer_kernel, count),
        out_shape=pltpu.VMEM((rows, features), jnp.bfloat16),
        in_specs=[hbm] * 12,
        out_specs=vmem,
        scratch_shapes=[
            pltpu.SMEM(block_table.shape, block_table.dtype),
            pltpu.SMEM(cache_lengths.shape, cache_lengths.dtype),
            pltpu.VMEM(parents.shape, parents.dtype),
            pltpu.VMEM(ids.shape, ids.dtype),
            pltpu.VMEM(weights_of.shape, weights_of.dtype),
            pltpu.VMEM(queries.shape, queries.dtype),
            pltpu.VMEM(tree_kv.shape, tree_kv.dtype),
            pltpu.VMEM(kv_cache.shape, kv_cache.dtype),
            pltpu.VMEM(w_out.shape, w_out.dtype),
            pltpu.VMEM((2, *w_gate.shape[1:]), w_gate.dtype),
            pltpu.VMEM((2, *w_up.shape[1:]), w_up.dtype),
            pltpu.VMEM((2, *w_down.shape[1:]), w_down.dtype),
            pltpu.VMEM((slices, rows, queries.shape[1]), jnp.bfloat16),
            pltpu.VMEM((1 << starts[1], rows, features), jnp.float32),
            pltpu.VMEM((CHUNKS, places, rows, front), jnp.bfloat16),
            pltpu.VMEM((places, rows, lanes), jnp.float32),
            pltpu.VMEM((2, tiles, tile_rows, LANES), jnp.float32),
            pltpu.VMEM((2, tiles, tile_rows, hidden_width), jnp.float32),
            pltpu.VMEM((2, tiles, tile_rows, hidden_width), jnp.float32),
            pltpu.VMEM((2, tiles, tile_rows, hidden_width), jnp.bfloat16),
            pltpu.VMEM((1 << starts[-2], rows, features), jnp.float32),
            pltpu.VMEM((CHUNKS, slices, rows, front), jnp.bfloat16),
            pltpu.VMEM((CHUNKS, slices, rows, front), jnp.bfloat16),
            pltpu.VMEM((len(BACK), places - 1, rows, back), jnp.bfloat16),
            pltpu.VMEM((len(BACK), places - 1, rows, back), jnp.bfloat16),
            dma((11 + CHUNKS,)),
            dma((4,)),
            dma((CHUNKS, 2)),
            dma((CHUNKS, len(groups) - 1)),
            dma((len(groups),)),
            dma((len(BACK), len(groups))),
            dma((3,)),
            dma((3,)),
        ],
        compiler_params=pltpu.CompilerParams(
            collective_id=0, has_side_effects=True, vmem_limit_bytes=60 << 20
        ),
    )(
        block_table,
        cache_lengths,
        queries,
        tree_kv,
        kv_cache,
        parents,
        w_out,
        w_gate,
        w_up,
        w_down,
        ids,
        weights_of,
    )


def solution(mesh):
    placed = (
        P(("groups", "wide"), None),
        P(None, ("groups", "wide"), None),
        P(None, ("groups", "wide"), None, None),
        P(("groups", "wide"), None),
        P(("groups", "wide"), None),
        P(("groups", "wide"), None),
        P("wide", None),
        P("wide", None, None),
        P("wide", None, None),
        P("wide", None, None),
        P(("groups", "wide"), None),
        P(("groups", "wide"), None),
    )
    return jax.shard_map(
        body, mesh=mesh, in_specs=placed, out_specs=P(("groups", "wide"), None), check_vma=False
    )
```
